128 devices in a mesh: bricks: 32 (over z, y, core), slab: 4 (over x).
Axes of the slice: x: 4, y: 4, z: 4, core: 2. Of those that a mesh axis runs over, the one named last changes fastest.
Arguments:
- observed: float32 [32, 64, 16, 128], P('bricks', 'slab'), may hold values from -6 to 6
- estimate: float32 [32, 64, 16, 128], P('bricks', 'slab'), may hold values from -6 to 6
- blur_taps: float32 [3, 15], replicated, may hold values from 0.02 to 0.15
- slot_brick: int32 [32], replicated, may hold values from 0 to 31, as said below
- neighbours: int32 [32, 6], replicated, may hold values from -1 to 31, as said below
- coords: int32 [32, 3], replicated, may hold values from 0 to 3, as said below
Outputs:
- solution: float32 [32, 64, 16, 128], P('bricks', 'slab')
- residual: float32 [32, 64, 16, 128], P('bricks', 'slab')
The draws below stay inside these ranges and needn't reach their ends.
Inputs may be any that keep to these rules, and one draw needn't show every extreme that they name: `slot_brick`: each brick number appears in exactly one row. neighbours[i, k] is the brick whose coords differ from brick i's by one along face k (order -z, +z, -y, +y, -x, +x), or -1 where no active brick sits there. `coords`: distinct positions, column 0 below 4, column 1 below 4, column 2 below 4.
All inputs are finite; a program needn't handle non-finite values.
Results may differ from the reference program's by a relative error of at most 0.0003.
Values sent between devices are 32-bit elements; how exact they have to be, the bound alone decides.
A program may use at most 64 MiB of HBM per device.

```python
import math
import jax
import jax.numpy as jnp
from jax import lax

BZ = 64
BY = 16
BX = 128
TAPS = 15
CG_STEPS = 2
GZ = 4
GY = 4
GX = 4
NB = 32


def brick_layout(key):
    base = jax.random.fold_in(key, 7)
    order = jax.random.permutation(jax.random.fold_in(base, 1), NB).astype(jnp.int32)
    lowest = jax.random.randint(jax.random.fold_in(base, 2), (), 0, GZ - 1).astype(jnp.int32)
    flip_y = jax.random.randint(jax.random.fold_in(base, 3), (), 0, 2).astype(jnp.int32)
    flip_x = jax.random.randint(jax.random.fold_in(base, 4), (), 0, 2).astype(jnp.int32)
    rows = jnp.arange(NB, dtype=jnp.int32)
    halves = rows // (NB // 2)
    within = rows % (NB // 2)
    layer = within // (2 * GX)
    spot = within % (2 * GX)
    row_y = halves + 2 * (spot // GX)
    col_x = spot % GX
    row_y = jnp.where(flip_y == 1, GY - 1 - row_y, row_y)
    col_x = jnp.where(flip_x == 1, GX - 1 - col_x, col_x)
    layer_z = lowest + layer
    by_row = jnp.stack([layer_z, row_y, col_x], axis=1).astype(jnp.int32)
    coords = jnp.zeros((NB, 3), jnp.int32).at[order].set(by_row)
    brick_ids = jnp.arange(NB, dtype=jnp.int32)
    limits = (GZ, GY, GX)
    linked = []
    for dimension in range(3):
        for offset in (-1, 1):
            target = coords.at[:, dimension].add(offset)
            inside = (target[:, dimension] >= 0) & (target[:, dimension] < limits[dimension])
            same_spot = jnp.all(coords[None, :, :] == target[:, None, :], axis=2)
            present = jnp.any(same_spot, axis=1) & inside
            linked.append(jnp.where(present, jnp.sum(jnp.where(same_spot, brick_ids[None, :], 0), axis=1), -1))
    return (order, coords, jnp.stack(linked, axis=1).astype(jnp.int32))


def draw_slot_brick(key, part):
    return brick_layout(key)[0]


def draw_neighbours(key, part):
    return brick_layout(key)[2]


def draw_coords(key, part):
    return brick_layout(key)[1]


def steps_of(own_key, shape, cuts, low, top_value):
    loudness = 1.0
    for dim, shards_of in cuts:
        draws = jax.random.uniform(jax.random.fold_in(jax.random.fold_in(own_key, 6), dim), (shards_of,), jnp.float32, low / len(cuts), top_value / len(cuts))
        loudness = loudness * jnp.repeat(jnp.exp(draws), shape[dim] // shards_of).reshape((-1,) + (1,) * (len(shape) - 1 - dim))
    return loudness


def bell_draw(rng, shape, width, most, split=(), held_as=jnp.bfloat16):
    gain = steps_of(rng, shape, split, -0.22, 0.18) if split else 1.0
    drawn = jax.random.normal(rng, shape, jnp.float32) * width * gain
    return jnp.minimum(jnp.maximum(drawn, -most), most).astype(held_as)


def setup_inputs(seed: int = 0) -> dict:
    seeds = jax.random.split(jax.random.key(seed), 7)
    observed = bell_draw(seeds[0], (NB, BZ, BY, BX), 1.0, 6.0, ((0, 32), (1, 4)), jnp.float32)
    estimate = bell_draw(seeds[1], (NB, BZ, BY, BX), 1.0, 6.0, ((0, 32), (1, 4)), jnp.float32)
    blur_taps = jnp.clip(jnp.exp(jax.random.uniform(seeds[2], (3, TAPS), jnp.float32, math.log(0.02), math.log(0.15))), 0.02, 0.15)
    slot_brick = draw_slot_brick(jax.random.fold_in(seeds[6], 71), 0)
    neighbours = draw_neighbours(jax.random.fold_in(seeds[6], 71), 0)
    coords = draw_coords(jax.random.fold_in(seeds[6], 71), 0)
    return {"observed": observed, "estimate": estimate, "blur_taps": blur_taps, "slot_brick": slot_brick, "neighbours": neighbours, "coords": coords}


SHRINK = 0.5
WEIGHT = 0.3


def neighbour_rows(slot_brick, neighbours):
    brick_ids = jnp.arange(slot_brick.shape[0], dtype=jnp.int32)
    row_of = jnp.sum(jnp.where(slot_brick[None, :] == brick_ids[:, None], brick_ids[None, :], 0), axis=1).astype(jnp.int32)
    linked = jnp.take(neighbours, slot_brick, axis=0)
    return jnp.where(linked >= 0, jnp.take(row_of, jnp.maximum(linked, 0)), -1).astype(jnp.int32)


def extend(volume, peer_rows, dimension, halo_width):
    extent = volume.shape[dimension]
    lower = peer_rows[:, 2 * (dimension - 1)]
    upper = peer_rows[:, 2 * (dimension - 1) + 1]
    top_layers = lax.slice_in_dim(volume, extent - halo_width, extent, axis=dimension)
    bottom_layers = lax.slice_in_dim(volume, 0, halo_width, axis=dimension)
    under_halo = jnp.take(top_layers, jnp.maximum(lower, 0), axis=0) * (lower >= 0).astype(volume.dtype).reshape(-1, 1, 1, 1)
    over_halo = jnp.take(bottom_layers, jnp.maximum(upper, 0), axis=0) * (upper >= 0).astype(volume.dtype).reshape(-1, 1, 1, 1)
    return jnp.concatenate([under_halo, volume, over_halo], axis=dimension)


def convolve(padded, kernel, dimension, extent, flipped):
    length = kernel.shape[0]
    summed = None
    for offset in range(length):
        weight = kernel[length - 1 - offset] if flipped else kernel[offset]
        shifted = weight * lax.slice_in_dim(padded, offset, offset + extent, axis=dimension)
        summed = shifted if summed is None else summed + shifted
    return summed


def blur_forward(volume, peer_rows, blur_taps):
    reach = blur_taps.shape[1] // 2
    for dimension in (1, 2, 3):
        volume = convolve(extend(volume, peer_rows, dimension, reach), blur_taps[dimension - 1], dimension, volume.shape[dimension], False)
    return volume


def blur_adjoint(volume, peer_rows, blur_taps):
    reach = blur_taps.shape[1] // 2
    for dimension in (3, 2, 1):
        volume = convolve(extend(volume, peer_rows, dimension, reach), blur_taps[dimension - 1], dimension, volume.shape[dimension], True)
    return volume


def shrink_gap(values):
    return -SHRINK * values / (values * values + SHRINK)


def identity_map(values):
    return values


def smooth(volume, peer_rows, penalty):
    summed = None
    for dimension in (1, 2, 3):
        extent = volume.shape[dimension]
        padded = extend(volume, peer_rows, dimension, 1)
        before = lax.slice_in_dim(padded, 0, extent, axis=dimension)
        beyond = lax.slice_in_dim(padded, 2, extent + 2, axis=dimension)
        has_lower = (peer_rows[:, 2 * (dimension - 1)] >= 0).astype(volume.dtype).reshape(-1, 1, 1, 1)
        position = lax.broadcasted_iota(jnp.int32, volume.shape, dimension)
        keep_low = jnp.where(position == 0, has_lower, 1.0)
        part_sum = penalty(volume - before) * keep_low - penalty(beyond - volume)
        summed = part_sum if summed is None else summed + part_sum
    return summed


def reference(observed, estimate, blur_taps, slot_brick, neighbours, coords):
    peer_rows = neighbour_rows(slot_brick, neighbours)
    layer_z = jnp.take(coords[:, 0], slot_brick)
    depth_cells = (layer_z[:, None] * BZ + jnp.arange(BZ, dtype=jnp.int32)[None, :]).astype(jnp.float32)
    damping = jnp.exp(-depth_cells / (BZ * GZ)).reshape(-1, BZ, 1, 1)
    blurred = blur_forward(estimate, peer_rows, blur_taps)
    residual = blur_adjoint(damping * observed - damping * damping * blurred, peer_rows, blur_taps) + WEIGHT * smooth(estimate, peer_rows, shrink_gap)
    direction = residual
    solution = estimate
    norm_now = jnp.sum(residual * residual)
    for cg_step in range(CG_STEPS):
        applied = blur_adjoint(damping * damping * blur_forward(direction, peer_rows, blur_taps), peer_rows, blur_taps) + WEIGHT * smooth(direction, peer_rows, identity_map)
        step_len = norm_now / jnp.sum(direction * applied)
        solution = solution + step_len * direction
        residual = residual - step_len * applied
        if cg_step + 1 < CG_STEPS:
            norm_next = jnp.sum(residual * residual)
            direction = residual + (norm_next / norm_now) * direction
            norm_now = norm_next
    return solution, residual
```

```python
import jax
import jax.numpy as jnp
from jax import lax
from jax.experimental import pallas as pl
from jax.experimental.pallas import tpu as pltpu
from jax.sharding import PartitionSpec as P

NB = 32
ND = 128
TAPS = 15
REACH = 7
SHRINK = 0.5
WEIGHT = 0.3
MESH = pl.DeviceIdType.MESH
f32 = jnp.float32
bf16 = jnp.bfloat16

EXCHANGES = {
    "est": 2, "obs": 2, "t1": 2, "t2": 2, "t3": 2, "t4": 2, "t5": 4, "t6": 2, "t7": 4,
    "b0": 2, "b1": 2,
}
NAMES = list(EXCHANGES)


def kernel(slot, links, coords, taps, obs_ref, est_ref, sol_ref, res_ref, *scratch):
    n = len(NAMES)
    send = dict(zip(NAMES, scratch[:n]))
    recv = dict(zip(NAMES, scratch[n : 2 * n]))
    (fields, work, gathered, weights_hi, weights_lo, planes0, planes1, planes2, smooth_sum,
     damp, source, peers, row_of, send_sems, recv_sems, plane_send, plane_recv) = scratch[2 * n :]
    planes = (planes0, planes1, planes2)
    ssem = {name: send_sems.at[k] for k, name in enumerate(NAMES)}
    rsem = {name: recv_sems.at[k] for k, name in enumerate(NAMES)}

    my_row = lax.axis_index("bricks")
    my_slab = lax.axis_index("slab")
    me = my_row * 4 + my_slab
    my_z, my_y, my_core = my_row // 8, lax.rem(my_row // 2, 4), lax.rem(my_row, 2)
    slabs = [lax.rem(my_slab + d, 4) for d in range(4)]
    cores = [my_core, 1 - my_core]

    def far_first(j):
        return 2 + j - (j // 2) * (2 * j - 1)

    def everyone(visit):
        def group(step, carry):
            z = lax.rem(my_z + far_first(step // 4), 4)
            y = lax.rem(my_y + far_first(lax.rem(step, 4)), 4)
            for d in (2, 1, 3, 0):
                for c in (0, 1):
                    row = (z * 4 + y) * 2 + cores[c]
                    visit(row * 4 + slabs[d], (row, slabs[d]))
            return carry

        lax.fori_loop(0, 15, group, 0)
        for d in (2, 1, 3, 0):
            for c in (1, 0):
                if d or c:
                    row = (my_z * 4 + my_y) * 2 + cores[c]
                    visit(row * 4 + slabs[d], (row, slabs[d]))

    def start(name):
        rows = EXCHANGES[name]
        src, dst = send[name], recv[name]

        def part(ref, k):
            return ref.at[pl.ds(pl.multiple_of(rows * k, rows), rows)]

        def visit(number, device):
            pltpu.make_async_remote_copy(
                src_ref=part(src, number), dst_ref=part(dst, me), send_sem=ssem[name],
                recv_sem=rsem[name], device_id=device, device_id_type=MESH,
            ).start()

        everyone(visit)
        pltpu.make_async_copy(part(src, me), part(dst, me), rsem[name]).start()

    def arrive(name):
        dst = recv[name]
        pltpu.make_async_copy(dst, dst, rsem[name]).wait()

    barrier = pltpu.get_barrier_semaphore()

    def greet(number, device):
        pl.semaphore_signal(barrier, inc=1, device_id=device, device_id_type=MESH)

    everyone(greet)

    for h in range(2):
        block = est_ref[0, 8 * h : 8 * h + 8].reshape(128, 128)
        send["est"][pl.ds(h, 128, stride=2), :] = block.T
        send["obs"][pl.ds(h, 128, stride=2), :] = obs_ref[0, 8 * h : 8 * h + 8].reshape(128, 128)
    pl.semaphore_wait(barrier, ND - 1)
    start("est")

    zero = jnp.zeros((8, 128), f32)
    for ref in (fields.at[0], fields.at[1], fields.at[2], work,
                *(planes[op].at[side] for op in range(3) for side in range(2))):
        ref[NB] = zero

    def find_row(brick, carry):
        row = jnp.int32(0)
        for r in range(NB):
            row = jnp.where(slot[r] == brick, r, row)
        row_of[brick] = row
        return carry

    lax.fori_loop(0, NB, find_row, 0)

    def find_peers(row, carry):
        brick = slot[row]
        for k in range(6):
            link = links[brick, k]
            peers[row, k] = jnp.where(link >= 0, row_of[jnp.maximum(link, 0)], NB)
        return carry

    lax.fori_loop(0, NB, find_peers, 0)

    sub = lax.broadcasted_iota(jnp.int32, (8, 128), 0)
    lane = lax.broadcasted_iota(jnp.int32, (8, 128), 1)
    in_y = lax.rem(lane, 16)

    def make_weights(slot_at, axis, flipped):
        a = lax.broadcasted_iota(jnp.int32, (128, 128), 1)
        b = lax.broadcasted_iota(jnp.int32, (128, 128), 0)
        for side in range(3):
            if axis == 0:
                tap = 8 * (side - 1) + a // 16 - b // 16 + REACH
                fits = lax.rem(a, 16) == lax.rem(b, 16)
            elif axis == 1:
                tap = 16 * (side - 1) + lax.rem(a, 16) - lax.rem(b, 16) + REACH
                fits = a // 16 == b // 16
            else:
                tap = 128 * (side - 1) + a - b + REACH
                fits = a >= 0
            if flipped:
                tap = TAPS - 1 - tap
            tap = jnp.where(fits, tap, -1)

            def pick(t, total):
                return jnp.where(tap == t, taps[axis, t], total)

            block = lax.fori_loop(0, TAPS, pick, jnp.zeros((128, 128), f32))
            high = block.astype(bf16)
            low = (block - high.astype(f32)).astype(bf16)
            cols = pl.ds(128 * side, 128)
            weights_hi[slot_at, :, cols] = high
            weights_lo[slot_at, :, cols] = low

    make_weights(0, 0, False)
    make_weights(1, 1, False)

    def bricks_loop(body):
        def step(g, carry):
            for u in range(8):
                body(g * 8 + u)
            return carry

        lax.fori_loop(0, 4, step, 0)

    def gather(ref, axis):
        def body(b):
            own = ref[b]
            lower = ref[peers[b, 2 * axis]]
            upper = ref[peers[b, 2 * axis + 1]]
            if axis == 0:
                lower = pltpu.roll(jnp.where(sub == 7, lower, own), 1, 0)
                upper = pltpu.roll(jnp.where(sub == 0, upper, own), 7, 0)
            gathered[b, :, 0:128] = lower
            gathered[b, :, 128:256] = own
            gathered[b, :, 256:384] = upper

        bricks_loop(body)

    def split(values):
        high = values.astype(bf16)
        return high, (values - high.astype(f32)).astype(bf16)

    NT = (((1,), (1,)), ((), ()))

    def apply(ref, axis, which):
        gather(ref, axis)
        high, low = split(gathered[...].reshape(256, 384))
        w_high, w_low = weights_hi[which], weights_lo[which]
        return (
            lax.dot_general(high, w_high, NT, preferred_element_type=f32)
            + lax.dot_general(low, w_high, NT, preferred_element_type=f32)
            + lax.dot_general(high, w_low, NT, preferred_element_type=f32)
        )

    def apply_turned(ref, axis, which):
        gather(ref, axis)
        high, low = split(gathered[...].reshape(256, 384))
        w_high, w_low = weights_hi[which], weights_lo[which]
        return (
            lax.dot_general(w_high, high, NT, preferred_element_type=f32)
            + lax.dot_general(w_high, low, NT, preferred_element_type=f32)
            + lax.dot_general(w_low, high, NT, preferred_element_type=f32)
        )

    def post(name, turned):
        rows = EXCHANGES[name]
        for h in range(2):
            send[name][pl.ds(h, 128, stride=rows), :] = turned[:, 128 * h : 128 * h + 128]

    def unpack(name, ref):
        rows = EXCHANGES[name]
        for h in range(2):
            block = recv[name][pl.ds(h, 128, stride=rows), :].T
            ref[16 * h : 16 * h + 16] = block.reshape(16, 8, 128)

    def plane_copies(op):
        copies = []
        for side, shift in ((0, 1), (1, ND - 1)):
            other = lax.rem(me + shift, ND)
            copies.append(
                pltpu.make_async_remote_copy(
                    src_ref=fields.at[op, pl.ds(0, NB)],
                    dst_ref=planes[op].at[side, pl.ds(0, NB)],
                    send_sem=plane_send.at[op, side], recv_sem=plane_recv.at[op, side],
                    device_id=(other // 4, lax.rem(other, 4)), device_id_type=MESH,
                )
            )
        return copies

    def around(op, b):
        field = fields.at[op]
        own = field[b]
        z_low, z_high, y_low, y_high = (field[peers[b, k]] for k in range(4))
        down = pltpu.roll(jnp.where(sub == 7, z_low, own), 1, 0)
        up = pltpu.roll(jnp.where(sub == 0, z_high, own), 7, 0)
        before_z = pltpu.roll(jnp.where(lane >= 112, down, own), 16, 1)
        beyond_z = pltpu.roll(jnp.where(lane < 16, up, own), 112, 1)
        before_y = pltpu.roll(jnp.where(in_y == 15, pltpu.roll(y_low, 112, 1), own), 1, 1)
        beyond_y = pltpu.roll(jnp.where(in_y == 0, pltpu.roll(y_high, 16, 1), own), 127, 1)
        before_x = planes[op][0, jnp.where(me == 0, peers[b, 4], b)]
        beyond_x = planes[op][1, jnp.where(me == ND - 1, peers[b, 5], b)]
        has = [jnp.where(peers[b, 2 * k] < NB, 1.0, 0.0) for k in range(3)]
        low_z = jnp.where((sub == 0) & (lane < 16), has[0], 1.0)
        low_y = jnp.where(in_y == 0, has[1], 1.0)
        low_x = jnp.where(me == 0, has[2], 1.0)
        return own, ((before_z, beyond_z, low_z), (before_y, beyond_y, low_y),
                     (before_x, beyond_x, low_x))

    def smooth_shrunk(op):
        def penalty(g):
            return -SHRINK * g / (g * g + SHRINK)

        def body(b):
            own, sides = around(op, b)
            total = zero
            for before, beyond, low in sides:
                total = total + penalty(own - before) * low - penalty(beyond - own)
            smooth_sum[b] = WEIGHT * total

        bricks_loop(body)

    def smooth_linear(op):
        def body(b):
            own, sides = around(op, b)
            total = zero
            for before, beyond, low in sides:
                total = total + (own - before) * low - (beyond - own)
            smooth_sum[b] = WEIGHT * total

        bricks_loop(body)

    def operate(op, out, to_zy, to_x, first, note=None, before_x=None, meanwhile=None):
        planes_moving = plane_copies(op)
        work[0:NB] = apply(fields.at[op], 0, 0).reshape(NB, 8, 128)
        post(to_zy, apply_turned(work, 1, 1))
        if note is not None:
            note()
        start(to_zy)
        for copy in planes_moving:
            copy.start()
        if before_x is not None:
            before_x()
        arrive(to_zy)
        unpack(to_zy, work)
        blurred = apply(work, 2, 2).reshape(NB, 8, 128)
        weighted = damp[...] * damp[...] * blurred
        work[0:NB] = source[...] - weighted if first else weighted
        post(to_x, apply_turned(work, 2, 3))
        start(to_x)
        for copy in planes_moving:
            copy.wait()
        if first:
            smooth_shrunk(op)
        else:
            smooth_linear(op)
        if meanwhile is not None:
            meanwhile()
        arrive(to_x)
        unpack(to_x, work)
        work[0:NB] = apply(work, 1, 4).reshape(NB, 8, 128)
        return apply(work, 0, 5).reshape(NB, 8, 128) + smooth_sum[...]

    arrive("est")
    fields[0, 0:NB] = recv["est"][...].reshape(NB, 8, 128)

    def prepare():
        start("obs")
        make_weights(2, 2, False)
        make_weights(3, 2, True)

        def body(b):
            depth = coords[slot[b], 0] * 64 + 8 * sub + me // 16
            damp[b] = jnp.exp(-depth.astype(f32) / 256.0)

        bricks_loop(body)
        arrive("obs")
        source[...] = damp[...] * recv["obs"][...].reshape(NB, 8, 128)

    def prepare_adjoint():
        make_weights(4, 1, True)
        make_weights(5, 0, True)

    fields[1, 0:NB] = operate(0, 1, "t1", "t2", True, before_x=prepare, meanwhile=prepare_adjoint)

    def send_r0():
        send["b0"][...] = fields[1, 0:NB].reshape(256, 128)
        start("b0")

    fields[2, 0:NB] = operate(1, 2, "t3", "t4", False, before_x=send_r0)

    def note_sums():
        r0, w1 = fields[1, 0:NB].reshape(256, 128), fields[2, 0:NB].reshape(256, 128)
        for k, product in ((2, r0 * r0), (3, r0 * w1)):
            total = jnp.sum(product, axis=0, keepdims=True)
            send["t5"][pl.ds(k, 128, stride=4), :] = jnp.broadcast_to(total, (128, 128))

    def send_w1():
        send["b1"][...] = fields[2, 0:NB].reshape(256, 128)
        start("b1")

    w2 = operate(2, None, "t5", "t6", False, note=note_sums, before_x=send_w1).reshape(256, 128)

    def total_of(rows):
        return jnp.sum(rows, keepdims=True)

    rr = total_of(recv["t5"][pl.ds(2, 128, stride=4), :])
    r0w1 = total_of(recv["t5"][pl.ds(3, 128, stride=4), :])
    step1 = rr / r0w1

    work[0:NB] = w2.reshape(NB, 8, 128)
    r0, w1 = fields[1, 0:NB].reshape(256, 128), fields[2, 0:NB].reshape(256, 128)
    r1 = r0 - step1 * w1
    ar1 = w1 - step1 * w2
    low_half = lax.broadcasted_iota(jnp.int32, (1, 128), 1) < 64

    def two_sums(first, second):
        a = jnp.sum(first, axis=0, keepdims=True)
        b = jnp.sum(second, axis=0, keepdims=True)
        a = a + pltpu.roll(a, 64, 1)
        b = b + pltpu.roll(b, 64, 1)
        return jnp.broadcast_to(jnp.where(low_half, a, b), (128, 128))

    w2_rows = w2.reshape(128, 2, 128)
    for h in range(2):
        send["t7"][pl.ds(h, 128, stride=4), :] = w2_rows[:, h, :]
    send["t7"][pl.ds(2, 128, stride=4), :] = two_sums(r1 * r1, r1 * ar1)
    send["t7"][pl.ds(3, 128, stride=4), :] = two_sums(r1 * w1, r0 * ar1)
    start("t7")
    arrive("b0")
    arrive("b1")
    arrive("t7")
    low = lax.broadcasted_iota(jnp.int32, (128, 128), 1) < 64
    row2 = recv["t7"][pl.ds(2, 128, stride=4), :]
    row3 = recv["t7"][pl.ds(3, 128, stride=4), :]
    rr1 = total_of(jnp.where(low, row2, 0.0))
    r1ar1 = total_of(jnp.where(low, 0.0, row2))
    cross = total_of(row3)
    ratio = rr1 / rr
    step2 = rr1 / (r1ar1 + ratio * cross + ratio * ratio * r0w1)
    for h in range(2):
        b0 = recv["b0"][pl.ds(h, 128, stride=2), :].T
        b1 = recv["b1"][pl.ds(h, 128, stride=2), :].T
        b2 = recv["t7"][pl.ds(h, 128, stride=4), :].T
        r = b0 - step1 * b1
        ar = b1 - step1 * b2
        est = est_ref[0, 8 * h : 8 * h + 8].reshape(128, 128)
        sol = est + step1 * b0 + step2 * (r + ratio * b0)
        res = r - step2 * (ar + ratio * b1)
        sol_ref[0, 8 * h : 8 * h + 8] = sol.reshape(8, 16, 128)
        res_ref[0, 8 * h : 8 * h + 8] = res.reshape(8, 16, 128)

    for name in NAMES:
        sent = send[name].at[pl.ds(0, 127 * EXCHANGES[name])]
        pltpu.make_async_copy(sent, sent, ssem[name]).wait()


def shards(observed, estimate, blur_taps, slot_brick, neighbours, coords):
    smem = pl.BlockSpec(memory_space=pltpu.SMEM)
    vmem = pl.BlockSpec(memory_space=pltpu.VMEM)
    shape = jax.ShapeDtypeStruct(estimate.shape, f32)
    buffers = [pltpu.VMEM((ND * EXCHANGES[name], 128), f32) for name in NAMES]
    count = len(NAMES)
    return pl.pallas_call(
        kernel,
        out_shape=(shape, shape),
        in_specs=[smem] * 4 + [vmem] * 2,
        out_specs=(vmem, vmem),
        scratch_shapes=buffers + buffers + [
            pltpu.VMEM((3, NB + 1, 8, 128), f32),
            pltpu.VMEM((NB + 1, 8, 128), f32),
            pltpu.VMEM((NB, 8, 384), f32),
            pltpu.VMEM((6, 128, 384), bf16),
            pltpu.VMEM((6, 128, 384), bf16),
            *[pltpu.VMEM((2, NB + 1, 8, 128), f32)] * 3,
            pltpu.VMEM((NB, 8, 128), f32),
            pltpu.VMEM((NB, 8, 128), f32),
            pltpu.VMEM((NB, 8, 128), f32),
            pltpu.SMEM((NB, 6), jnp.int32),
            pltpu.SMEM((NB,), jnp.int32),
            pltpu.SemaphoreType.DMA((count,)),
            pltpu.SemaphoreType.DMA((count,)),
            pltpu.SemaphoreType.DMA((3, 2)),
            pltpu.SemaphoreType.DMA((3, 2)),
        ],
        compiler_params=pltpu.CompilerParams(collective_id=0, has_side_effects=True),
        name="splitting_step",
    )(slot_brick, neighbours, coords, blur_taps, observed, estimate)


def solution(mesh):
    split = P("bricks", "slab", None, None)
    return jax.shard_map(
        shards,
        mesh=mesh,
        in_specs=(split, split, P(), P(), P(), P()),
        out_specs=(split, split),
        check_vma=False,
    )
```

```python
import jax
import jax.numpy as jnp
from jax import lax
from jax.experimental import pallas as pl
from jax.experimental.pallas import tpu as pltpu
from jax.sharding import PartitionSpec as P

NB = 32
ND = 128
TAPS = 15
REACH = 7
SHRINK = 0.5
WEIGHT = 0.3
MESH = pl.DeviceIdType.MESH
f32 = jnp.float32
bf16 = jnp.bfloat16

EXCHANGES = {
    "est": (2, 2, "from"), "obs": (2, 2, "from"), "t1": (2, 2, ""), "t2": (2, 2, ""),
    "t3": (2, 2, ""), "t4": (2, 2, ""), "t5": (2, 2, ""), "t6": (2, 2, ""),
    "t7": (3, 4, "to"), "b0": (2, 2, "to"), "b1": (2, 2, "to"), "sums": (1, 1, ""),
}
NAMES = list(EXCHANGES)


def kernel(slot_in, links_in, coords_in, taps_in, obs_in, est_in, sol_ref, res_ref, *scratch):
    n = len(NAMES)
    send = dict(zip(NAMES, scratch[:n]))
    recv = dict(zip(NAMES, scratch[n : 2 * n]))
    (fields, work, gathered, weights_hi, weights_lo, planes0, planes1, planes2, smooth_sum,
     damp, source, peers, row_of, send_sems, recv_sems, plane_send, plane_recv, slot, links,
     coords, taps, obs_ref, est_ref, load_sems) = scratch[2 * n :]
    planes = (planes0, planes1, planes2)
    ssem = {name: send_sems.at[k] for k, name in enumerate(NAMES)}
    rsem = {name: recv_sems.at[k] for k, name in enumerate(NAMES)}

    my_row = lax.axis_index("bricks")
    my_slab = lax.axis_index("slab")
    me = my_row // 2 * 8 + my_slab * 2 + lax.rem(my_row, 2)
    my_brick = my_row * 4 + my_slab
    my_z, my_y, my_core = my_row // 8, lax.rem(my_row // 2, 4), lax.rem(my_row, 2)
    slabs = [lax.rem(my_slab + d, 4) for d in range(4)]
    cores = [my_core, 1 - my_core]

    def far_first(j):
        return 2 + j - (j // 2) * (2 * j - 1)

    def everyone(visit):
        def group(step, carry):
            z = lax.rem(my_z + far_first(step // 4), 4)
            y = lax.rem(my_y + far_first(lax.rem(step, 4)), 4)
            for d in (2, 1, 3, 0):
                for c in (0, 1):
                    row = (z * 4 + y) * 2 + cores[c]
                    number = ((z * 4 + y) * 4 + slabs[d]) * 2 + cores[c]
                    visit(number, row * 4 + slabs[d], (row, slabs[d]))
            return carry

        lax.fori_loop(0, 15, group, 0)
        for d in (2, 1, 3, 0):
            for c in (1, 0):
                if d or c:
                    row = (my_z * 4 + my_y) * 2 + cores[c]
                    number = ((my_z * 4 + my_y) * 4 + slabs[d]) * 2 + cores[c]
                    visit(number, row * 4 + slabs[d], (row, slabs[d]))

    def start(name):
        rows, pitch, bricks = EXCHANGES[name]
        src, dst = send[name], recv[name]
        from_me = my_brick if bricks == "from" else me
        to_me = my_brick if bricks == "to" else me

        def part(ref, k):
            return ref.at[pl.ds(pl.multiple_of(pitch * k, pitch), rows)]

        def visit(number, place, device):
            pltpu.make_async_remote_copy(
                src_ref=part(src, place if bricks == "to" else number),
                dst_ref=part(dst, from_me), send_sem=ssem[name], recv_sem=rsem[name],
                device_id=device, device_id_type=MESH,
            ).start()

        everyone(visit)
        pltpu.make_async_copy(part(src, to_me), part(dst, from_me), rsem[name]).start()

    def arrive(name):
        dst = recv[name].at[pl.ds(0, ND * EXCHANGES[name][0])]
        pltpu.make_async_copy(dst, dst, rsem[name]).wait()

    barrier = pltpu.get_barrier_semaphore()

    def greet(number, place, device):
        pl.semaphore_signal(barrier, inc=1, device_id=device, device_id_type=MESH)

    everyone(greet)
    loads = [
        pltpu.make_async_copy(src, dst, load_sems.at[k])
        for k, (src, dst) in enumerate(
            ((est_in, est_ref), (obs_in, obs_ref), (slot_in, slot), (links_in, links),
             (coords_in, coords), (taps_in, taps)))
    ]
    for load in loads:
        load.start()
    for load in loads[:2]:
        load.wait()
    for h in range(2):
        block = est_ref[0, 8 * h : 8 * h + 8].reshape(128, 128)
        send["est"][pl.ds(h, 128, stride=2), :] = block.T
        send["obs"][pl.ds(h, 128, stride=2), :] = obs_ref[0, 8 * h : 8 * h + 8].reshape(128, 128)
    pl.semaphore_wait(barrier, ND - 1)
    start("est")
    start("obs")
    for load in loads[2:]:
        load.wait()

    zero = jnp.zeros((8, 128), f32)
    for ref in (fields.at[0], fields.at[1], fields.at[2], work,
                *(planes[op].at[side] for op in range(3) for side in range(2))):
        ref[NB] = zero

    def find_row(brick, carry):
        row = jnp.int32(0)
        for r in range(NB):
            row = jnp.where(slot[r] == brick, r, row)
        row_of[brick] = row
        return carry

    lax.fori_loop(0, NB, find_row, 0)

    def find_peers(row, carry):
        brick = slot[row]
        for k in range(6):
            link = links[k, brick]
            peers[row, k] = jnp.where(link >= 0, row_of[jnp.maximum(link, 0)], NB)
        return carry

    lax.fori_loop(0, NB, find_peers, 0)

    sub = lax.broadcasted_iota(jnp.int32, (8, 128), 0)
    lane = lax.broadcasted_iota(jnp.int32, (8, 128), 1)
    in_y = lax.rem(lane, 16)

    def make_weights(slot_at, axis, flipped):
        a = lax.broadcasted_iota(jnp.int32, (128, 128), 1)
        b = lax.broadcasted_iota(jnp.int32, (128, 128), 0)
        for side in range(3):
            if axis == 0:
                tap = 8 * (side - 1) + a // 16 - b // 16 + REACH
                fits = lax.rem(a, 16) == lax.rem(b, 16)
            elif axis == 1:
                tap = 16 * (side - 1) + lax.rem(a, 16) - lax.rem(b, 16) + REACH
                fits = a // 16 == b // 16
            else:
                tap = 128 * (side - 1) + a - b + REACH
                fits = a >= 0
            if flipped:
                tap = TAPS - 1 - tap
            tap = jnp.where(fits, tap, -1)

            def pick(t, total):
                return jnp.where(tap == t, taps[axis, t], total)

            block = lax.fori_loop(0, TAPS, pick, jnp.zeros((128, 128), f32))
            high = block.astype(bf16)
            low = (block - high.astype(f32)).astype(bf16)
            cols = pl.ds(128 * side, 128)
            weights_hi[slot_at, :, cols] = high
            weights_lo[slot_at, :, cols] = low

    make_weights(0, 0, False)
    make_weights(1, 1, False)

    def bricks_loop(body):
        def step(g, carry):
            for u in range(8):
                body(g * 8 + u)
            return carry

        lax.fori_loop(0, 4, step, 0)

    def gather(ref, axis):
        def body(b):
            own = ref[b]
            lower = ref[peers[b, 2 * axis]]
            upper = ref[peers[b, 2 * axis + 1]]
            if axis == 0:
                lower = pltpu.roll(jnp.where(sub == 7, lower, own), 1, 0)
                upper = pltpu.roll(jnp.where(sub == 0, upper, own), 7, 0)
            gathered[b, :, 0:128] = lower
            gathered[b, :, 128:256] = own
            gathered[b, :, 256:384] = upper

        bricks_loop(body)

    def split(values):
        high = values.astype(bf16)
        return high, (values - high.astype(f32)).astype(bf16)

    NT = (((1,), (1,)), ((), ()))

    def apply(ref, axis, which):
        gather(ref, axis)
        high, low = split(gathered[...].reshape(256, 384))
        w_high, w_low = weights_hi[which], weights_lo[which]
        return (
            lax.dot_general(high, w_high, NT, preferred_element_type=f32)
            + lax.dot_general(low, w_high, NT, preferred_element_type=f32)
            + lax.dot_general(high, w_low, NT, preferred_element_type=f32)
        )

    def apply_turned(ref, axis, which):
        gather(ref, axis)
        high, low = split(gathered[...].reshape(256, 384))
        w_high, w_low = weights_hi[which], weights_lo[which]
        return (
            lax.dot_general(w_high, high, NT, preferred_element_type=f32)
            + lax.dot_general(w_high, low, NT, preferred_element_type=f32)
            + lax.dot_general(w_low, high, NT, preferred_element_type=f32)
        )

    def post(name, turned):
        rows = EXCHANGES[name][1]
        for h in range(2):
            send[name][pl.ds(h, 128, stride=rows), :] = turned[:, 128 * h : 128 * h + 128]

    def unpack(name, ref):
        rows = EXCHANGES[name][1]
        for h in range(2):
            block = recv[name][pl.ds(h, 128, stride=rows), :].T
            ref[16 * h : 16 * h + 16] = block.reshape(16, 8, 128)

    def plane_copies(op):
        copies = []
        for side, shift in ((0, 1), (1, ND - 1)):
            other = lax.rem(me + shift, ND)
            chip, core = other // 2, lax.rem(other, 2)
            copies.append(
                pltpu.make_async_remote_copy(
                    src_ref=fields.at[op, pl.ds(0, NB)],
                    dst_ref=planes[op].at[side, pl.ds(0, NB)],
                    send_sem=plane_send.at[op, side], recv_sem=plane_recv.at[op, side],
                    device_id=(chip // 4 * 2 + core, lax.rem(chip, 4)),
                    device_id_type=MESH,
                )
            )
        return copies

    def around(op, b):
        field = fields.at[op]
        own = field[b]
        z_low, z_high, y_low, y_high = (field[peers[b, k]] for k in range(4))
        down = pltpu.roll(jnp.where(sub == 7, z_low, own), 1, 0)
        up = pltpu.roll(jnp.where(sub == 0, z_high, own), 7, 0)
        before_z = pltpu.roll(jnp.where(lane >= 112, down, own), 16, 1)
        beyond_z = pltpu.roll(jnp.where(lane < 16, up, own), 112, 1)
        before_y = pltpu.roll(jnp.where(in_y == 15, pltpu.roll(y_low, 112, 1), own), 1, 1)
        beyond_y = pltpu.roll(jnp.where(in_y == 0, pltpu.roll(y_high, 16, 1), own), 127, 1)
        before_x = planes[op][0, jnp.where(me == 0, peers[b, 4], b)]
        beyond_x = planes[op][1, jnp.where(me == ND - 1, peers[b, 5], b)]
        has = [jnp.where(peers[b, 2 * k] < NB, 1.0, 0.0) for k in range(3)]
        low_z = jnp.where((sub == 0) & (lane < 16), has[0], 1.0)
        low_y = jnp.where(in_y == 0, has[1], 1.0)
        low_x = jnp.where(me == 0, has[2], 1.0)
        return own, ((before_z, beyond_z, low_z), (before_y, beyond_y, low_y),
                     (before_x, beyond_x, low_x))

    def smooth_shrunk(op):
        def penalty(g):
            return -SHRINK * g / (g * g + SHRINK)

        def body(b):
            own, sides = around(op, b)
            total = zero
            for before, beyond, low in sides:
                total = total + penalty(own - before) * low - penalty(beyond - own)
            smooth_sum[b] = WEIGHT * total

        bricks_loop(body)

    def smooth_linear(op):
        def body(b):
            own, sides = around(op, b)
            total = zero
            for before, beyond, low in sides:
                total = total + (own - before) * low - (beyond - own)
            smooth_sum[b] = WEIGHT * total

        bricks_loop(body)

    def operate(op, out, to_zy, to_x, first, before_x=None, meanwhile=None):
        planes_moving = plane_copies(op)
        for copy in planes_moving:
            copy.start()
        work[0:NB] = apply(fields.at[op], 0, 0).reshape(NB, 8, 128)
        post(to_zy, apply_turned(work, 1, 1))
        start(to_zy)
        if before_x is not None:
            before_x()
        arrive(to_zy)
        unpack(to_zy, work)
        blurred = apply(work, 2, 2).reshape(NB, 8, 128)
        weighted = damp[...] * damp[...] * blurred
        work[0:NB] = source[...] - weighted if first else weighted
        post(to_x, apply_turned(work, 2, 3))
        start(to_x)
        for copy in planes_moving:
            copy.wait()
        if first:
            smooth_shrunk(op)
        else:
            smooth_linear(op)
        if meanwhile is not None:
            meanwhile()
        arrive(to_x)
        unpack(to_x, work)
        work[0:NB] = apply(work, 1, 4).reshape(NB, 8, 128)
        return apply(work, 0, 5).reshape(NB, 8, 128) + smooth_sum[...]

    arrive("est")
    fields[0, 0:NB] = recv["est"][...].reshape(NB, 8, 128)

    def prepare():
        make_weights(2, 2, False)
        make_weights(3, 2, True)

        def body(b):
            depth = coords[0, slot[b]] * 64 + 8 * sub + me // 16
            damp[b] = jnp.exp(-depth.astype(f32) / 256.0)

        bricks_loop(body)
        arrive("obs")
        source[...] = damp[...] * recv["obs"][...].reshape(NB, 8, 128)

    def prepare_adjoint():
        make_weights(4, 1, True)
        make_weights(5, 0, True)

    fields[1, 0:NB] = operate(0, 1, "t1", "t2", True, before_x=prepare, meanwhile=prepare_adjoint)

    def send_r0():
        send["b0"][...] = fields[1, 0:NB].reshape(256, 128)
        start("b0")

    fields[2, 0:NB] = operate(1, 2, "t3", "t4", False, before_x=send_r0)

    low_half = lax.broadcasted_iota(jnp.int32, (1, 128), 1) < 64

    def two_sums(first, second):
        a = jnp.sum(first, axis=0, keepdims=True)
        b = jnp.sum(second, axis=0, keepdims=True)
        a = a + pltpu.roll(a, 64, 1)
        b = b + pltpu.roll(b, 64, 1)
        return jnp.where(low_half, a, b)

    def send_w1():
        r0, w1 = fields[1, 0:NB].reshape(256, 128), fields[2, 0:NB].reshape(256, 128)
        send["sums"][...] = jnp.broadcast_to(two_sums(r0 * r0, r0 * w1), (128, 128))
        start("sums")
        send["b1"][...] = w1
        start("b1")

    w2 = operate(2, None, "t5", "t6", False, before_x=send_w1).reshape(256, 128)

    def total_of(rows):
        return jnp.sum(rows, keepdims=True)

    low = lax.broadcasted_iota(jnp.int32, (128, 128), 1) < 64
    arrive("sums")
    rr = total_of(jnp.where(low, recv["sums"][...], 0.0))
    r0w1 = total_of(jnp.where(low, 0.0, recv["sums"][...]))
    step1 = rr / r0w1

    work[0:NB] = w2.reshape(NB, 8, 128)
    r0, w1 = fields[1, 0:NB].reshape(256, 128), fields[2, 0:NB].reshape(256, 128)
    r1 = r0 - step1 * w1
    ar1 = w1 - step1 * w2
    first_pair = two_sums(r1 * r1, r1 * ar1)
    second_pair = two_sums(r1 * w1, r0 * ar1)
    quarter = lax.rem(lax.broadcasted_iota(jnp.int32, (1, 128), 1), 64) < 32
    first_pair = first_pair + pltpu.roll(first_pair, 96, 1)
    second_pair = second_pair + pltpu.roll(second_pair, 32, 1)
    sums = jnp.where(quarter, first_pair, second_pair)
    w2_rows = w2.reshape(128, 2, 128)
    for h in range(2):
        send["t7"][pl.ds(h, 128, stride=4), :] = w2_rows[:, h, :]
    send["t7"][pl.ds(2, 128, stride=4), :] = jnp.broadcast_to(sums, (128, 128))
    start("t7")
    arrive("b0")
    arrive("b1")
    arrive("t7")
    sums = recv["t7"][pl.ds(2, 128, stride=4), :]
    lane_of = lax.broadcasted_iota(jnp.int32, (128, 128), 1)
    own = lax.rem(lane_of, 64) < 32
    rr1 = total_of(jnp.where(own & low, sums, 0.0))
    r1ar1 = total_of(jnp.where(own & (lane_of >= 64), sums, 0.0))
    cross = total_of(jnp.where(own, 0.0, sums))
    ratio = rr1 / rr
    step2 = rr1 / (r1ar1 + ratio * cross + ratio * ratio * r0w1)
    for h in range(2):
        b0 = recv["b0"][pl.ds(h, 128, stride=2), :].T
        b1 = recv["b1"][pl.ds(h, 128, stride=2), :].T
        b2 = recv["t7"][pl.ds(h, 128, stride=4), :].T
        r = b0 - step1 * b1
        ar = b1 - step1 * b2
        est = est_ref[0, 8 * h : 8 * h + 8].reshape(128, 128)
        sol = est + step1 * b0 + step2 * (r + ratio * b0)
        res = r - step2 * (ar + ratio * b1)
        sol_ref[0, 8 * h : 8 * h + 8] = sol.reshape(8, 16, 128)
        res_ref[0, 8 * h : 8 * h + 8] = res.reshape(8, 16, 128)

    for name in NAMES:
        sent = send[name].at[pl.ds(0, (ND - 1) * EXCHANGES[name][0])]
        pltpu.make_async_copy(sent, sent, ssem[name]).wait()


def shards(observed, estimate, blur_taps, slot_brick, neighbours, coords):
    place = pl.BlockSpec(memory_space=pl.ANY)
    vmem = pl.BlockSpec(memory_space=pltpu.VMEM)
    shape = jax.ShapeDtypeStruct(estimate.shape, f32)
    buffers = [pltpu.VMEM((ND * EXCHANGES[name][1], 128), f32) for name in NAMES]
    count = len(NAMES)
    return pl.pallas_call(
        kernel,
        out_shape=(shape, shape),
        in_specs=[place] * 6,
        out_specs=(vmem, vmem),
        scratch_shapes=buffers + buffers + [
            pltpu.VMEM((3, NB + 1, 8, 128), f32),
            pltpu.VMEM((NB + 1, 8, 128), f32),
            pltpu.VMEM((NB, 8, 384), f32),
            pltpu.VMEM((6, 128, 384), bf16),
            pltpu.VMEM((6, 128, 384), bf16),
            *[pltpu.VMEM((2, NB + 1, 8, 128), f32)] * 3,
            pltpu.VMEM((NB, 8, 128), f32),
            pltpu.VMEM((NB, 8, 128), f32),
            pltpu.VMEM((NB, 8, 128), f32),
            pltpu.SMEM((NB, 6), jnp.int32),
            pltpu.SMEM((NB,), jnp.int32),
            pltpu.SemaphoreType.DMA((count,)),
            pltpu.SemaphoreType.DMA((count,)),
            pltpu.SemaphoreType.DMA((3, 2)),
            pltpu.SemaphoreType.DMA((3, 2)),
            pltpu.SMEM((NB,), jnp.int32),
            pltpu.SMEM((6, NB), jnp.int32),
            pltpu.SMEM((3, NB), jnp.int32),
            pltpu.SMEM((3, TAPS), f32),
            pltpu.VMEM(observed.shape, f32),
            pltpu.VMEM(estimate.shape, f32),
            pltpu.SemaphoreType.DMA((6,)),
        ],
        compiler_params=pltpu.CompilerParams(collective_id=0, has_side_effects=True),
        name="splitting_step",
    )(slot_brick, neighbours.T, coords.T, blur_taps, observed, estimate)


def solution(mesh):
    split = P("bricks", "slab", None, None)
    return jax.shard_map(
        shards,
        mesh=mesh,
        in_specs=(split, split, P(), P(), P(), P()),
        out_specs=(split, split),
        check_vma=False,
    )
```

```python
import jax
import jax.numpy as jnp
from jax import lax
from jax.experimental import pallas as pl
from jax.experimental.pallas import tpu as pltpu
from jax.sharding import PartitionSpec as P

NB = 32
ND = 128
TAPS = 15
REACH = 7
SHRINK = 0.5
WEIGHT = 0.3
MESH = pl.DeviceIdType.MESH
f32 = jnp.float32
bf16 = jnp.bfloat16

EXCHANGES = {
    "est": (2, 2, "from"), "obs": (2, 2, "from"), "t1": (2, 2, ""), "t2": (2, 2, ""),
    "t3": (2, 2, ""), "t4": (2, 2, ""), "t5": (2, 2, ""), "t6": (2, 2, ""),
    "t7": (2, 2, "to"), "b0": (2, 2, "to"), "b1": (2, 2, "to"), "sums1": (1, 1, ""),
    "sums2": (1, 1, ""),
}
NAMES = list(EXCHANGES)


def kernel(slot_in, links_in, coords_in, taps_in, obs_in, est_in, sol_ref, res_ref, *scratch):
    n = len(NAMES)
    send = dict(zip(NAMES, scratch[:n]))
    recv = dict(zip(NAMES, scratch[n : 2 * n]))
    (fields, work, gathered, weights_hi, weights_lo, blocks, planes0, planes1, planes2, smooth_sum,
     damp, source, peers, row_of, send_sems, recv_sems, plane_send, plane_recv, slot, links,
     coords, taps, obs_ref, est_ref, load_sems, partly) = scratch[2 * n :]
    planes = (planes0, planes1, planes2)
    ssem = {name: send_sems.at[k] for k, name in enumerate(NAMES)}
    rsem = {name: recv_sems.at[k] for k, name in enumerate(NAMES)}

    my_row = lax.axis_index("bricks")
    my_slab = lax.axis_index("slab")
    me = my_row // 2 * 8 + my_slab * 2 + lax.rem(my_row, 2)
    my_brick = my_row * 4 + my_slab
    my_z, my_y, my_core = my_row // 8, lax.rem(my_row // 2, 4), lax.rem(my_row, 2)
    slabs = [lax.rem(my_slab + d, 4) for d in range(4)]
    cores = [my_core, 1 - my_core]

    def far_first(j):
        return 2 + j - (j // 2) * (2 * j - 1)

    def everyone(visit):
        def group(step, carry):
            z = lax.rem(my_z + far_first(step // 4), 4)
            y = lax.rem(my_y + far_first(lax.rem(step, 4)), 4)
            for d in (2, 1, 3, 0):
                for c in (0, 1):
                    row = (z * 4 + y) * 2 + cores[c]
                    number = ((z * 4 + y) * 4 + slabs[d]) * 2 + cores[c]
                    visit(number, row * 4 + slabs[d], (row, slabs[d]))
            return carry

        lax.fori_loop(0, 15, group, 0)
        for d in (2, 1, 3, 0):
            for c in (1, 0):
                if d or c:
                    row = (my_z * 4 + my_y) * 2 + cores[c]
                    number = ((my_z * 4 + my_y) * 4 + slabs[d]) * 2 + cores[c]
                    visit(number, row * 4 + slabs[d], (row, slabs[d]))

    def start(name):
        rows, pitch, bricks = EXCHANGES[name]
        src, dst = send[name], recv[name]
        from_me = my_brick if bricks == "from" else me
        to_me = my_brick if bricks == "to" else me

        def part(ref, k):
            return ref.at[pl.ds(pl.multiple_of(pitch * k, pitch), rows)]

        def visit(number, place, device):
            pltpu.make_async_remote_copy(
                src_ref=part(src, place if bricks == "to" else number),
                dst_ref=part(dst, from_me), send_sem=ssem[name], recv_sem=rsem[name],
                device_id=device, device_id_type=MESH,
            ).start()

        everyone(visit)
        pltpu.make_async_copy(part(src, to_me), part(dst, from_me), rsem[name]).start()

    def arrive(name):
        dst = recv[name].at[pl.ds(0, ND * EXCHANGES[name][0])]
        pltpu.make_async_copy(dst, dst, rsem[name]).wait()

    barrier = pltpu.get_barrier_semaphore()

    def greet(number, place, device):
        pl.semaphore_signal(barrier, inc=1, device_id=device, device_id_type=MESH)

    everyone(greet)
    loads = [
        pltpu.make_async_copy(src, dst, load_sems.at[k])
        for k, (src, dst) in enumerate(
            ((est_in, est_ref), (obs_in, obs_ref), (slot_in, slot), (links_in, links),
             (coords_in, coords), (taps_in, taps)))
    ]
    for load in loads:
        load.start()
    for load in loads[:2]:
        load.wait()
    for h in range(2):
        block = est_ref[0, 8 * h : 8 * h + 8].reshape(128, 128)
        send["est"][pl.ds(h, 128, stride=2), :] = block.T
        send["obs"][pl.ds(h, 128, stride=2), :] = obs_ref[0, 8 * h : 8 * h + 8].reshape(128, 128)
    pl.semaphore_wait(barrier, ND - 1)
    start("est")
    start("obs")
    for load in loads[2:]:
        load.wait()

    zero = jnp.zeros((8, 128), f32)
    for ref in (fields.at[0], fields.at[1], fields.at[2], work,
                *(planes[op].at[side] for op in range(3) for side in range(2))):
        ref[NB] = zero

    def find_row(brick, carry):
        row = jnp.int32(0)
        for r in range(NB):
            row = jnp.where(slot[r] == brick, r, row)
        row_of[brick] = row
        return carry

    lax.fori_loop(0, NB, find_row, 0)

    def find_peers(row, carry):
        brick = slot[row]
        for k in range(6):
            link = links[k, brick]
            peers[row, k] = jnp.where(link >= 0, row_of[jnp.maximum(link, 0)], NB)
        return carry

    lax.fori_loop(0, NB, find_peers, 0)

    sub = lax.broadcasted_iota(jnp.int32, (8, 128), 0)
    lane = lax.broadcasted_iota(jnp.int32, (8, 128), 1)
    in_y = lax.rem(lane, 16)

    def make_weights(slot_at, axis, flipped, keep=None):
        a = lax.broadcasted_iota(jnp.int32, (128, 128), 1)
        b = lax.broadcasted_iota(jnp.int32, (128, 128), 0)
        for side in range(3):
            if axis == 0:
                tap = 8 * (side - 1) + a // 16 - b // 16 + REACH
                fits = lax.rem(a, 16) == lax.rem(b, 16)
            elif axis == 1:
                tap = 16 * (side - 1) + lax.rem(a, 16) - lax.rem(b, 16) + REACH
                fits = a // 16 == b // 16
            else:
                tap = 128 * (side - 1) + a - b + REACH
                fits = a >= 0
            if flipped:
                tap = TAPS - 1 - tap
            tap = jnp.where(fits, tap, -1)

            def pick(t, total):
                return jnp.where(tap == t, taps[axis, t], total)

            block = lax.fori_loop(0, TAPS, pick, jnp.zeros((128, 128), f32))
            if keep is not None:
                blocks[keep, side] = block
            if slot_at is not None:
                hold_weights(slot_at, side, block)

    def hold_weights(slot_at, at, block):
        high = block.astype(bf16)
        weights_hi[slot_at, :, 128 * at : 128 * at + 128] = high
        weights_lo[slot_at, :, 128 * at : 128 * at + 128] = (block - high.astype(f32)).astype(bf16)

    def both_x_passes(slot_at):
        def through(back, forth):
            return jnp.dot(blocks[1, back], blocks[0, forth], precision=lax.Precision.HIGHEST,
                           preferred_element_type=f32)

        hold_weights(slot_at, 0, through(1, 0) + through(0, 1))
        hold_weights(slot_at, 1, through(1, 1))
        hold_weights(slot_at, 2, through(1, 2) + through(2, 1))
        hold_weights(slot_at, 3, through(0, 2) + through(2, 0))

    make_weights(0, 0, False)
    make_weights(1, 1, False)

    def bricks_loop(body):
        def step(g, carry):
            for u in range(8):
                body(g * 8 + u)
            return carry

        lax.fori_loop(0, 4, step, 0)

    def gather(ref, axis, ends=False):
        for b in range(NB):
            own = ref[b]
            lower = ref[peers[b, 2 * axis]]
            upper = ref[peers[b, 2 * axis + 1]]
            if axis == 0:
                lower = pltpu.roll(jnp.where(sub == 7, lower, own), 1, 0)
                upper = pltpu.roll(jnp.where(sub == 0, upper, own), 7, 0)
            gathered[b, :, 0:128] = lower
            gathered[b, :, 128:256] = own
            gathered[b, :, 256:384] = upper
            if ends:
                has_lower = jnp.where(peers[b, 4] < NB, 1.0, 0.0)
                has_upper = jnp.where(peers[b, 5] < NB, 1.0, 0.0)
                inner = jnp.where(lane >= 128 - REACH, own * has_upper, 0.0)
                gathered[b, :, 384:512] = jnp.where(lane < REACH, own * has_lower, inner)

    def split(values):
        high = values.astype(bf16)
        return high, (values - high.astype(f32)).astype(bf16)

    NT = (((1,), (1,)), ((), ()))

    def operands(ref, axis, which, ends):
        gather(ref, axis, ends)
        depth = 512 if ends else 384
        high, low = split(gathered[:, :, 0:depth].reshape(256, depth))
        return high, low, weights_hi[which, :, 0:depth], weights_lo[which, :, 0:depth]

    def dot(a, b):
        return lax.dot_general(a, b, NT, preferred_element_type=f32)

    def apply(ref, axis, which):
        high, low, w_high, w_low = operands(ref, axis, which, False)
        return dot(high, w_high) + dot(low, w_high) + dot(high, w_low)

    def apply_turned(ref, axis, which, ends=False):
        high, low, w_high, w_low = operands(ref, axis, which, ends)
        return dot(w_high, high) + dot(w_high, low) + dot(w_low, high)

    def post(name, turned):
        rows = EXCHANGES[name][1]
        for h in range(2):
            send[name][pl.ds(h, 128, stride=rows), :] = turned[:, 128 * h : 128 * h + 128]

    def unpack(name, ref, scale=None):
        rows = EXCHANGES[name][1]
        for h in range(2):
            block = recv[name][pl.ds(h, 128, stride=rows), :].T
            block = block.reshape(16, 8, 128)
            if scale is not None:
                block = block * scale[16 * h : 16 * h + 16]
            ref[16 * h : 16 * h + 16] = block

    def plane_copies(op):
        copies = []
        for side, shift in ((0, 1), (1, ND - 1)):
            other = lax.rem(me + shift, ND)
            chip, core = other // 2, lax.rem(other, 2)
            copies.append(
                pltpu.make_async_remote_copy(
                    src_ref=fields.at[op, pl.ds(0, NB)],
                    dst_ref=planes[op].at[side, pl.ds(0, NB)],
                    send_sem=plane_send.at[op, side], recv_sem=plane_recv.at[op, side],
                    device_id=(chip // 4 * 2 + core, lax.rem(chip, 4)),
                    device_id_type=MESH,
                )
            )
        return copies

    def around(op, b):
        field = fields.at[op]
        own = field[b]
        z_low, z_high, y_low, y_high = (field[peers[b, k]] for k in range(4))
        down = pltpu.roll(jnp.where(sub == 7, z_low, own), 1, 0)
        up = pltpu.roll(jnp.where(sub == 0, z_high, own), 7, 0)
        before_z = pltpu.roll(jnp.where(lane >= 112, down, own), 16, 1)
        beyond_z = pltpu.roll(jnp.where(lane < 16, up, own), 112, 1)
        before_y = pltpu.roll(jnp.where(in_y == 15, pltpu.roll(y_low, 112, 1), own), 1, 1)
        beyond_y = pltpu.roll(jnp.where(in_y == 0, pltpu.roll(y_high, 16, 1), own), 127, 1)
        before_x = planes[op][0, jnp.where(me == 0, peers[b, 4], b)]
        beyond_x = planes[op][1, jnp.where(me == ND - 1, peers[b, 5], b)]
        has = [jnp.where(peers[b, 2 * k] < NB, 1.0, 0.0) for k in range(3)]
        low_z = jnp.where((sub == 0) & (lane < 16), has[0], 1.0)
        low_y = jnp.where(in_y == 0, has[1], 1.0)
        low_x = jnp.where(me == 0, has[2], 1.0)
        return own, ((before_z, beyond_z, low_z), (before_y, beyond_y, low_y),
                     (before_x, beyond_x, low_x))

    def smooth_shrunk(op):
        def penalty(g):
            return -SHRINK * g / (g * g + SHRINK)

        def body(b):
            own, sides = around(op, b)
            total = zero
            for before, beyond, low in sides:
                total = total + penalty(own - before) * low - penalty(beyond - own)
            smooth_sum[op, b] = WEIGHT * total

        bricks_loop(body)

    def smooth_linear(op):
        def body(b):
            own, sides = around(op, b)
            total = zero
            for before, beyond, low in sides:
                total = total + (own - before) * low - (beyond - own)
            smooth_sum[op, b] = WEIGHT * total

        bricks_loop(body)

    def operate(op, to_zy, to_x, first, before_x=None, meanwhile=None):
        planes_moving = plane_copies(op)
        work[0:NB] = apply(fields.at[op], 0, 0).reshape(NB, 8, 128)
        post(to_zy, apply_turned(work, 1, 1))
        start(to_zy)
        for copy in planes_moving:
            copy.start()
        if before_x is not None:
            before_x()
        arrive(to_zy)
        unpack(to_zy, work, damp)
        turned = apply_turned(work, 2, 2, ends=True)
        post(to_x, source[...] - turned if first else turned)
        start(to_x)
        for copy in planes_moving:
            copy.wait()
        if first:
            smooth_shrunk(op)
        else:
            smooth_linear(op)
        if meanwhile is not None:
            meanwhile()
        arrive(to_x)
        unpack(to_x, work)
        work[0:NB] = apply(work, 1, 4).reshape(NB, 8, 128)
        return apply(work, 0, 5).reshape(NB, 8, 128) + smooth_sum[op]

    arrive("est")
    fields[0, 0:NB] = recv["est"][...].reshape(NB, 8, 128)

    def prepare():
        make_weights(None, 2, False, keep=0)
        make_weights(3, 2, True, keep=1)
        both_x_passes(2)

        def body(b):
            depth = coords[0, slot[b]] * 64 + 8 * sub + me // 16
            damp[b] = jnp.exp(-depth.astype(f32) / 256.0)

        bricks_loop(body)
        arrive("obs")
        work[0:NB] = damp[...] * recv["obs"][...].reshape(NB, 8, 128)
        source[...] = apply_turned(work, 2, 3)
        damp[...] = damp[...] * damp[...]

    def prepare_adjoint():
        make_weights(4, 1, True)
        make_weights(5, 0, True)

    fields[1, 0:NB] = operate(0, "t1", "t2", True, before_x=prepare, meanwhile=prepare_adjoint)

    def send_r0():
        send["b0"][...] = fields[1, 0:NB].reshape(256, 128)
        start("b0")

    fields[2, 0:NB] = operate(1, "t3", "t4", False, before_x=send_r0)

    low_half = lax.broadcasted_iota(jnp.int32, (1, 128), 1) < 64

    def two_sums(first, second):
        a = jnp.sum(first, axis=0, keepdims=True)
        b = jnp.sum(second, axis=0, keepdims=True)
        a = a + pltpu.roll(a, 64, 1)
        b = b + pltpu.roll(b, 64, 1)
        return jnp.where(low_half, a, b)

    def send_w1():
        r0, w1 = fields[1, 0:NB].reshape(256, 128), fields[2, 0:NB].reshape(256, 128)
        send["sums1"][...] = jnp.broadcast_to(two_sums(r0 * r0, r0 * w1), (128, 128))
        start("sums1")
        send["b1"][...] = w1
        start("b1")

    def total_of(rows):
        return jnp.sum(rows, keepdims=True)

    lane_of = lax.broadcasted_iota(jnp.int32, (128, 128), 1)

    def first_step():
        arrive("sums1")
        rr = total_of(jnp.where(lane_of < 64, recv["sums1"][...], 0.0))
        r0w1 = total_of(jnp.where(lane_of < 64, 0.0, recv["sums1"][...]))
        return rr, r0w1, rr / r0w1

    def send_sums():
        rr, r0w1, step1 = first_step()
        r0, w1 = fields[1, 0:NB].reshape(256, 128), fields[2, 0:NB].reshape(256, 128)
        r1 = r0 - step1 * w1
        smooth1 = (smooth_sum[1] - step1 * smooth_sum[2]).reshape(256, 128)
        blurred = recv["t3"][...] - step1 * recv["t5"][...]
        passed = send["t4"][...] - step1 * send["t6"][...]
        first_pair = two_sums(r1 * r1, r1 * smooth1 + blurred * passed)
        second = jnp.sum(r1 * w1, axis=0, keepdims=True)
        for shift in (64, 32):
            second = second + pltpu.roll(second, shift, 1)
        first_pair = first_pair + pltpu.roll(first_pair, 96, 1)
        quarter = lax.rem(lax.broadcasted_iota(jnp.int32, (1, 128), 1), 64) < 32
        send["sums2"][...] = jnp.broadcast_to(jnp.where(quarter, first_pair, second), (128, 128))
        start("sums2")
        steps.extend((rr, r0w1, step1))

    steps = []
    work_out = operate(2, "t5", "t6", False, before_x=send_w1, meanwhile=send_sums)
    send["t7"][...] = work_out.reshape(256, 128)
    start("t7")
    rr, r0w1, step1 = steps
    arrive("b0")
    arrive("b1")
    arrive("sums2")
    sums = recv["sums2"][...]
    inner = lax.rem(lane_of, 64) < 32
    rr1 = total_of(jnp.where(inner & (lane_of < 64), sums, 0.0))
    r1ar1 = total_of(jnp.where(inner & (lane_of >= 64), sums, 0.0))
    r1w1 = total_of(jnp.where(lane_of < 64, jnp.where(inner, 0.0, sums), 0.0))
    ratio = rr1 / rr
    step2 = rr1 / (r1ar1 + 2.0 * ratio * r1w1 + ratio * ratio * r0w1)
    for h in range(2):
        b0 = recv["b0"][pl.ds(h, 128, stride=2), :].T
        b1 = recv["b1"][pl.ds(h, 128, stride=2), :].T
        r = b0 - step1 * b1
        est = est_ref[0, 8 * h : 8 * h + 8].reshape(128, 128)
        sol = est + step1 * b0 + step2 * (r + ratio * b0)
        sol_ref[0, 8 * h : 8 * h + 8] = sol.reshape(8, 16, 128)
        partly[128 * h : 128 * h + 128] = r - step2 * (b1 + ratio * b1)
    arrive("t7")
    for h in range(2):
        b2 = recv["t7"][pl.ds(h, 128, stride=2), :].T
        res = partly[128 * h : 128 * h + 128] + step2 * step1 * b2
        res_ref[0, 8 * h : 8 * h + 8] = res.reshape(8, 16, 128)

    for name in NAMES:
        sent = send[name].at[pl.ds(0, (ND - 1) * EXCHANGES[name][0])]
        pltpu.make_async_copy(sent, sent, ssem[name]).wait()


def shards(observed, estimate, blur_taps, slot_brick, neighbours, coords):
    place = pl.BlockSpec(memory_space=pl.ANY)
    vmem = pl.BlockSpec(memory_space=pltpu.VMEM)
    shape = jax.ShapeDtypeStruct(estimate.shape, f32)
    buffers = [pltpu.VMEM((ND * EXCHANGES[name][1], 128), f32) for name in NAMES]
    count = len(NAMES)
    return pl.pallas_call(
        kernel,
        out_shape=(shape, shape),
        in_specs=[place] * 6,
        out_specs=(vmem, vmem),
        scratch_shapes=buffers + buffers + [
            pltpu.VMEM((3, NB + 1, 8, 128), f32),
            pltpu.VMEM((NB + 1, 8, 128), f32),
            pltpu.VMEM((NB, 8, 512), f32),
            pltpu.VMEM((6, 128, 512), bf16),
            pltpu.VMEM((6, 128, 512), bf16),
            pltpu.VMEM((2, 3, 128, 128), f32),
            *[pltpu.VMEM((2, NB + 1, 8, 128), f32)] * 3,
            pltpu.VMEM((3, NB, 8, 128), f32),
            pltpu.VMEM((NB, 8, 128), f32),
            pltpu.VMEM((128, 256), f32),
            pltpu.SMEM((NB, 6), jnp.int32),
            pltpu.SMEM((NB,), jnp.int32),
            pltpu.SemaphoreType.DMA((count,)),
            pltpu.SemaphoreType.DMA((count,)),
            pltpu.SemaphoreType.DMA((3, 2)),
            pltpu.SemaphoreType.DMA((3, 2)),
            pltpu.SMEM((NB,), jnp.int32),
            pltpu.SMEM((6, NB), jnp.int32),
            pltpu.SMEM((3, NB), jnp.int32),
            pltpu.SMEM((3, TAPS), f32),
            pltpu.VMEM(observed.shape, f32),
            pltpu.VMEM(estimate.shape, f32),
            pltpu.SemaphoreType.DMA((6,)),
            pltpu.VMEM((256, 128), f32),
        ],
        compiler_params=pltpu.CompilerParams(collective_id=0, has_side_effects=True),
        name="splitting_step",
    )(slot_brick, neighbours.T, coords.T, blur_taps, observed, estimate)


def solution(mesh):
    split = P("bricks", "slab", None, None)
    return jax.shard_map(
        shards,
        mesh=mesh,
        in_specs=(split, split, P(), P(), P(), P()),
        out_specs=(split, split),
        check_vma=False,
    )
```

```python
import jax
import jax.numpy as jnp
from jax import lax
from jax.experimental import pallas as pl
from jax.experimental.pallas import tpu as pltpu
from jax.sharding import PartitionSpec as P

NB = 32
ND = 128
TAPS = 15
REACH = 7
SHRINK = 0.5
WEIGHT = 0.3
MESH = pl.DeviceIdType.MESH
f32 = jnp.float32
bf16 = jnp.bfloat16

EXCHANGES = {
    "est": (2, 2, "from"), "obs": (2, 2, "from"), "t1": (2, 2, ""), "t2": (2, 2, ""),
    "t3": (2, 2, ""), "t4": (2, 2, ""), "t5": (2, 2, ""), "t6": (2, 2, ""),
    "t7": (2, 2, "to"), "b0": (2, 2, "to"), "b1": (2, 2, "to"), "sums1": (1, 1, ""),
    "sums2": (1, 1, ""),
}
NAMES = list(EXCHANGES)


def kernel(slot_in, links_in, coords_in, taps_in, obs_in, est_in, sol_ref, res_ref, *scratch):
    n = len(NAMES)
    send = dict(zip(NAMES, scratch[:n]))
    recv = dict(zip(NAMES, scratch[n : 2 * n]))
    (fields, work, gathered, weights, turned_weights, blocks, planes0, planes1, planes2, smooth_sum,
     damp, source, peers, row_of, send_sems, recv_sems, plane_send, plane_recv, slot, links,
     coords, taps, obs_ref, est_ref, load_sems, partly) = scratch[2 * n :]
    planes = (planes0, planes1, planes2)
    ssem = {name: send_sems.at[k] for k, name in enumerate(NAMES)}
    rsem = {name: recv_sems.at[k] for k, name in enumerate(NAMES)}

    my_row = lax.axis_index("bricks")
    my_slab = lax.axis_index("slab")
    me = my_row // 2 * 8 + my_slab * 2 + lax.rem(my_row, 2)
    my_brick = my_row * 4 + my_slab
    my_z, my_y, my_core = my_row // 8, lax.rem(my_row // 2, 4), lax.rem(my_row, 2)
    slabs = [lax.rem(my_slab + d, 4) for d in range(4)]
    cores = [my_core, 1 - my_core]

    def far_first(j):
        return 2 + j - (j // 2) * (2 * j - 1)

    def everyone(visit):
        def group(step, carry):
            z = lax.rem(my_z + far_first(step // 4), 4)
            y = lax.rem(my_y + far_first(lax.rem(step, 4)), 4)
            for d in (2, 1, 3, 0):
                for c in (0, 1):
                    row = (z * 4 + y) * 2 + cores[c]
                    number = ((z * 4 + y) * 4 + slabs[d]) * 2 + cores[c]
                    visit(number, row * 4 + slabs[d], (row, slabs[d]))
            return carry

        lax.fori_loop(0, 15, group, 0)
        for d in (2, 1, 3, 0):
            for c in (1, 0):
                if d or c:
                    row = (my_z * 4 + my_y) * 2 + cores[c]
                    number = ((my_z * 4 + my_y) * 4 + slabs[d]) * 2 + cores[c]
                    visit(number, row * 4 + slabs[d], (row, slabs[d]))

    def start(name):
        rows, pitch, bricks = EXCHANGES[name]
        src, dst = send[name], recv[name]
        from_me = my_brick if bricks == "from" else me
        to_me = my_brick if bricks == "to" else me

        def part(ref, k):
            return ref.at[pl.ds(pl.multiple_of(pitch * k, pitch), rows)]

        def visit(number, place, device):
            pltpu.make_async_remote_copy(
                src_ref=part(src, place if bricks == "to" else number),
                dst_ref=part(dst, from_me), send_sem=ssem[name], recv_sem=rsem[name],
                device_id=device, device_id_type=MESH,
            ).start()

        everyone(visit)
        pltpu.make_async_copy(part(src, to_me), part(dst, from_me), rsem[name]).start()

    def arrive(name):
        dst = recv[name].at[pl.ds(0, ND * EXCHANGES[name][0])]
        pltpu.make_async_copy(dst, dst, rsem[name]).wait()

    barrier = pltpu.get_barrier_semaphore()

    def greet(number, place, device):
        pl.semaphore_signal(barrier, inc=1, device_id=device, device_id_type=MESH)

    everyone(greet)
    loads = [
        pltpu.make_async_copy(src, dst, load_sems.at[k])
        for k, (src, dst) in enumerate(
            ((est_in, est_ref), (obs_in, obs_ref), (slot_in, slot), (links_in, links),
             (coords_in, coords), (taps_in, taps)))
    ]
    for load in loads:
        load.start()
    for load in loads[:2]:
        load.wait()
    for h in range(2):
        block = est_ref[0, 8 * h : 8 * h + 8].reshape(128, 128)
        send["est"][pl.ds(h, 128, stride=2), :] = block.T
        send["obs"][pl.ds(h, 128, stride=2), :] = obs_ref[0, 8 * h : 8 * h + 8].reshape(128, 128)
    pl.semaphore_wait(barrier, ND - 1)
    start("est")
    start("obs")
    for load in loads[2:]:
        load.wait()

    zero = jnp.zeros((8, 128), f32)
    for ref in (fields.at[0], fields.at[1], fields.at[2], work,
                *(planes[op].at[side] for op in range(3) for side in range(2))):
        ref[NB] = zero

    def find_row(brick, carry):
        row = jnp.int32(0)
        for r in range(NB):
            row = jnp.where(slot[r] == brick, r, row)
        row_of[brick] = row
        return carry

    lax.fori_loop(0, NB, find_row, 0)

    def find_peers(row, carry):
        brick = slot[row]
        for k in range(6):
            link = links[k, brick]
            peers[row, k] = jnp.where(link >= 0, row_of[jnp.maximum(link, 0)], NB)
        return carry

    lax.fori_loop(0, NB, find_peers, 0)

    sub = lax.broadcasted_iota(jnp.int32, (8, 128), 0)
    lane = lax.broadcasted_iota(jnp.int32, (8, 128), 1)
    in_y = lax.rem(lane, 16)

    def make_weights(slot_at, axis, flipped, turned=False, keep=None):
        a = lax.broadcasted_iota(jnp.int32, (128, 128), 1 if turned else 0)
        b = lax.broadcasted_iota(jnp.int32, (128, 128), 0 if turned else 1)
        for side in range(3):
            if axis == 0:
                tap = 8 * (side - 1) + a // 16 - b // 16 + REACH
                fits = lax.rem(a, 16) == lax.rem(b, 16)
            elif axis == 1:
                tap = 16 * (side - 1) + lax.rem(a, 16) - lax.rem(b, 16) + REACH
                fits = a // 16 == b // 16
            else:
                tap = 128 * (side - 1) + a - b + REACH
                fits = a >= 0
            if flipped:
                tap = TAPS - 1 - tap
            tap = jnp.where(fits, tap, -1)

            def pick(t, total):
                return jnp.where(tap == t, taps[axis, t], total)

            block = lax.fori_loop(0, TAPS, pick, jnp.zeros((128, 128), f32))
            if keep is not None:
                blocks[keep, side] = block
            if turned and slot_at is not None:
                hold_turned(slot_at, side, block)
            elif slot_at is not None:
                high = block.astype(bf16)
                rows = pl.ds(128 * side, 128)
                weights[slot_at, rows, 0:128] = high
                weights[slot_at, rows, 128:256] = (block - high.astype(f32)).astype(bf16)

    def hold_turned(slot_at, at, block):
        high = block.astype(bf16)
        cols = pl.ds(128 * at, 128)
        turned_weights[slot_at, 0:128, cols] = high
        turned_weights[slot_at, 128:256, cols] = (block - high.astype(f32)).astype(bf16)

    def both_x_passes(slot_at):
        def through(back, forth):
            return jnp.dot(blocks[1, back], blocks[0, forth], precision=lax.Precision.HIGHEST,
                           preferred_element_type=f32)

        hold_turned(slot_at, 0, through(1, 0) + through(0, 1))
        hold_turned(slot_at, 1, through(1, 1))
        hold_turned(slot_at, 2, through(1, 2) + through(2, 1))
        hold_turned(slot_at, 3, through(0, 2) + through(2, 0))

    make_weights(0, 0, False)
    make_weights(0, 1, False, turned=True)

    def bricks_loop(body):
        def step(g, carry):
            for u in range(8):
                body(g * 8 + u)
            return carry

        lax.fori_loop(0, 4, step, 0)

    def gather(ref, axis, ends=False):
        for b in range(NB):
            own = ref[b]
            lower = ref[peers[b, 2 * axis]]
            upper = ref[peers[b, 2 * axis + 1]]
            if axis == 0:
                lower = pltpu.roll(jnp.where(sub == 7, lower, own), 1, 0)
                upper = pltpu.roll(jnp.where(sub == 0, upper, own), 7, 0)
            gathered[b, :, 0:128] = lower
            gathered[b, :, 128:256] = own
            gathered[b, :, 256:384] = upper
            if ends:
                has_lower = jnp.where(peers[b, 4] < NB, 1.0, 0.0)
                has_upper = jnp.where(peers[b, 5] < NB, 1.0, 0.0)
                inner = jnp.where(lane >= 128 - REACH, own * has_upper, 0.0)
                gathered[b, :, 384:512] = jnp.where(lane < REACH, own * has_lower, inner)

    def split(values):
        high = values.astype(bf16)
        return high, (values - high.astype(f32)).astype(bf16)

    def operands(ref, axis, ends):
        gather(ref, axis, ends)
        depth = 512 if ends else 384
        return depth, *split(gathered[:, :, 0:depth].reshape(256, depth))

    def dot(a, b, contract):
        return lax.dot_general(a, b, (contract, ((), ())), preferred_element_type=f32)

    def apply(ref, axis, which):
        _, high, low = operands(ref, axis, False)
        both = dot(high, weights[which], ((1,), (0,)))
        rest = dot(low, weights[which, :, 0:128], ((1,), (0,)))
        return both[:, 0:128] + both[:, 128:256] + rest

    def apply_turned(ref, axis, which, ends=False):
        depth, high, low = operands(ref, axis, ends)
        both = dot(turned_weights[which, :, 0:depth], high, ((1,), (1,)))
        rest = dot(turned_weights[which, 0:128, 0:depth], low, ((1,), (1,)))
        return both[0:128] + both[128:256] + rest

    def post(name, turned):
        rows = EXCHANGES[name][1]
        for h in range(2):
            send[name][pl.ds(h, 128, stride=rows), :] = turned[:, 128 * h : 128 * h + 128]

    def unpack(name, ref, scale=None):
        rows = EXCHANGES[name][1]
        for h in range(2):
            block = recv[name][pl.ds(h, 128, stride=rows), :].T
            block = block.reshape(16, 8, 128)
            if scale is not None:
                block = block * scale[16 * h : 16 * h + 16]
            ref[16 * h : 16 * h + 16] = block

    def plane_copies(op):
        copies = []
        for side, shift in ((0, 1), (1, ND - 1)):
            other = lax.rem(me + shift, ND)
            chip, core = other // 2, lax.rem(other, 2)
            copies.append(
                pltpu.make_async_remote_copy(
                    src_ref=fields.at[op, pl.ds(0, NB)],
                    dst_ref=planes[op].at[side, pl.ds(0, NB)],
                    send_sem=plane_send.at[op, side], recv_sem=plane_recv.at[op, side],
                    device_id=(chip // 4 * 2 + core, lax.rem(chip, 4)),
                    device_id_type=MESH,
                )
            )
        return copies

    def around(op, b):
        field = fields.at[op]
        own = field[b]
        z_low, z_high, y_low, y_high = (field[peers[b, k]] for k in range(4))
        down = pltpu.roll(jnp.where(sub == 7, z_low, own), 1, 0)
        up = pltpu.roll(jnp.where(sub == 0, z_high, own), 7, 0)
        before_z = pltpu.roll(jnp.where(lane >= 112, down, own), 16, 1)
        beyond_z = pltpu.roll(jnp.where(lane < 16, up, own), 112, 1)
        before_y = pltpu.roll(jnp.where(in_y == 15, pltpu.roll(y_low, 112, 1), own), 1, 1)
        beyond_y = pltpu.roll(jnp.where(in_y == 0, pltpu.roll(y_high, 16, 1), own), 127, 1)
        before_x = planes[op][0, jnp.where(me == 0, peers[b, 4], b)]
        beyond_x = planes[op][1, jnp.where(me == ND - 1, peers[b, 5], b)]
        has = [jnp.where(peers[b, 2 * k] < NB, 1.0, 0.0) for k in range(3)]
        low_z = jnp.where((sub == 0) & (lane < 16), has[0], 1.0)
        low_y = jnp.where(in_y == 0, has[1], 1.0)
        low_x = jnp.where(me == 0, has[2], 1.0)
        return own, ((before_z, beyond_z, low_z), (before_y, beyond_y, low_y),
                     (before_x, beyond_x, low_x))

    def smooth_shrunk(op):
        def penalty(g):
            return -SHRINK * g / (g * g + SHRINK)

        def body(b):
            own, sides = around(op, b)
            total = zero
            for before, beyond, low in sides:
                total = total + penalty(own - before) * low - penalty(beyond - own)
            smooth_sum[op, b] = WEIGHT * total

        bricks_loop(body)

    def smooth_linear(op):
        def body(b):
            own, sides = around(op, b)
            total = zero
            for before, beyond, low in sides:
                total = total + (own - before) * low - (beyond - own)
            smooth_sum[op, b] = WEIGHT * total

        bricks_loop(body)

    def operate(op, to_zy, to_x, first, before_x=None, meanwhile=None):
        planes_moving = plane_copies(op)
        work[0:NB] = apply(fields.at[op], 0, 0).reshape(NB, 8, 128)
        post(to_zy, apply_turned(work, 1, 0))
        start(to_zy)
        for copy in planes_moving:
            copy.start()
        if before_x is not None:
            before_x()
        arrive(to_zy)
        unpack(to_zy, work, damp)
        turned = apply_turned(work, 2, 1, ends=True)
        post(to_x, source[...] - turned if first else turned)
        start(to_x)
        for copy in planes_moving:
            copy.wait()
        if first:
            smooth_shrunk(op)
        else:
            smooth_linear(op)
        if meanwhile is not None:
            meanwhile()
        arrive(to_x)
        unpack(to_x, work)
        work[0:NB] = apply(work, 1, 1).reshape(NB, 8, 128)
        return apply(work, 0, 2).reshape(NB, 8, 128) + smooth_sum[op]

    arrive("est")
    fields[0, 0:NB] = recv["est"][...].reshape(NB, 8, 128)

    def prepare():
        make_weights(None, 2, False, turned=True, keep=0)
        make_weights(2, 2, True, turned=True, keep=1)
        both_x_passes(1)

        def body(b):
            depth = coords[0, slot[b]] * 64 + 8 * sub + me // 16
            damp[b] = jnp.exp(-depth.astype(f32) / 256.0)

        bricks_loop(body)
        arrive("obs")
        work[0:NB] = damp[...] * recv["obs"][...].reshape(NB, 8, 128)
        source[...] = apply_turned(work, 2, 2)
        damp[...] = damp[...] * damp[...]

    def prepare_adjoint():
        make_weights(1, 1, True)
        make_weights(2, 0, True)

    fields[1, 0:NB] = operate(0, "t1", "t2", True, before_x=prepare, meanwhile=prepare_adjoint)

    def send_r0():
        send["b0"][...] = fields[1, 0:NB].reshape(256, 128)
        start("b0")

    fields[2, 0:NB] = operate(1, "t3", "t4", False, before_x=send_r0)

    low_half = lax.broadcasted_iota(jnp.int32, (1, 128), 1) < 64

    def two_sums(first, second):
        a = jnp.sum(first, axis=0, keepdims=True)
        b = jnp.sum(second, axis=0, keepdims=True)
        a = a + pltpu.roll(a, 64, 1)
        b = b + pltpu.roll(b, 64, 1)
        return jnp.where(low_half, a, b)

    def send_w1():
        r0, w1 = fields[1, 0:NB].reshape(256, 128), fields[2, 0:NB].reshape(256, 128)
        send["sums1"][...] = jnp.broadcast_to(two_sums(r0 * r0, r0 * w1), (128, 128))
        start("sums1")
        send["b1"][...] = w1
        start("b1")

    def total_of(rows):
        return jnp.sum(rows, keepdims=True)

    lane_of = lax.broadcasted_iota(jnp.int32, (128, 128), 1)

    def first_step():
        arrive("sums1")
        rr = total_of(jnp.where(lane_of < 64, recv["sums1"][...], 0.0))
        r0w1 = total_of(jnp.where(lane_of < 64, 0.0, recv["sums1"][...]))
        return rr, r0w1, rr / r0w1

    def send_sums():
        rr, r0w1, step1 = first_step()
        r0, w1 = fields[1, 0:NB].reshape(256, 128), fields[2, 0:NB].reshape(256, 128)
        r1 = r0 - step1 * w1
        smooth1 = (smooth_sum[1] - step1 * smooth_sum[2]).reshape(256, 128)
        blurred = recv["t3"][...] - step1 * recv["t5"][...]
        passed = send["t4"][...] - step1 * send["t6"][...]
        first_pair = two_sums(r1 * r1, r1 * smooth1 + blurred * passed)
        second = jnp.sum(r1 * w1, axis=0, keepdims=True)
        for shift in (64, 32):
            second = second + pltpu.roll(second, shift, 1)
        first_pair = first_pair + pltpu.roll(first_pair, 96, 1)
        quarter = lax.rem(lax.broadcasted_iota(jnp.int32, (1, 128), 1), 64) < 32
        send["sums2"][...] = jnp.broadcast_to(jnp.where(quarter, first_pair, second), (128, 128))
        start("sums2")
        steps.extend((rr, r0w1, step1))

    steps = []
    work_out = operate(2, "t5", "t6", False, before_x=send_w1, meanwhile=send_sums)
    send["t7"][...] = work_out.reshape(256, 128)
    start("t7")
    rr, r0w1, step1 = steps
    arrive("b0")
    arrive("b1")
    arrive("sums2")
    sums = recv["sums2"][...]
    inner = lax.rem(lane_of, 64) < 32
    rr1 = total_of(jnp.where(inner & (lane_of < 64), sums, 0.0))
    r1ar1 = total_of(jnp.where(inner & (lane_of >= 64), sums, 0.0))
    r1w1 = total_of(jnp.where(lane_of < 64, jnp.where(inner, 0.0, sums), 0.0))
    ratio = rr1 / rr
    step2 = rr1 / (r1ar1 + 2.0 * ratio * r1w1 + ratio * ratio * r0w1)
    for h in range(2):
        b0 = recv["b0"][pl.ds(h, 128, stride=2), :].T
        b1 = recv["b1"][pl.ds(h, 128, stride=2), :].T
        r = b0 - step1 * b1
        est = est_ref[0, 8 * h : 8 * h + 8].reshape(128, 128)
        sol = est + step1 * b0 + step2 * (r + ratio * b0)
        sol_ref[0, 8 * h : 8 * h + 8] = sol.reshape(8, 16, 128)
        partly[128 * h : 128 * h + 128] = r - step2 * (b1 + ratio * b1)
    arrive("t7")
    for h in range(2):
        b2 = recv["t7"][pl.ds(h, 128, stride=2), :].T
        res = partly[128 * h : 128 * h + 128] + step2 * step1 * b2
        res_ref[0, 8 * h : 8 * h + 8] = res.reshape(8, 16, 128)

    for name in NAMES:
        sent = send[name].at[pl.ds(0, (ND - 1) * EXCHANGES[name][0])]
        pltpu.make_async_copy(sent, sent, ssem[name]).wait()


def shards(observed, estimate, blur_taps, slot_brick, neighbours, coords):
    place = pl.BlockSpec(memory_space=pl.ANY)
    vmem = pl.BlockSpec(memory_space=pltpu.VMEM)
    shape = jax.ShapeDtypeStruct(estimate.shape, f32)
    buffers = [pltpu.VMEM((ND * EXCHANGES[name][1], 128), f32) for name in NAMES]
    count = len(NAMES)
    return pl.pallas_call(
        kernel,
        out_shape=(shape, shape),
        in_specs=[place] * 6,
        out_specs=(vmem, vmem),
        scratch_shapes=buffers + buffers + [
            pltpu.VMEM((3, NB + 1, 8, 128), f32),
            pltpu.VMEM((NB + 1, 8, 128), f32),
            pltpu.VMEM((NB, 8, 512), f32),
            pltpu.VMEM((3, 384, 256), bf16),
            pltpu.VMEM((3, 256, 512), bf16),
            pltpu.VMEM((2, 3, 128, 128), f32),
            *[pltpu.VMEM((2, NB + 1, 8, 128), f32)] * 3,
            pltpu.VMEM((3, NB, 8, 128), f32),
            pltpu.VMEM((NB, 8, 128), f32),
            pltpu.VMEM((128, 256), f32),
            pltpu.SMEM((NB, 6), jnp.int32),
            pltpu.SMEM((NB,), jnp.int32),
            pltpu.SemaphoreType.DMA((count,)),
            pltpu.SemaphoreType.DMA((count,)),
            pltpu.SemaphoreType.DMA((3, 2)),
            pltpu.SemaphoreType.DMA((3, 2)),
            pltpu.SMEM((NB,), jnp.int32),
            pltpu.SMEM((6, NB), jnp.int32),
            pltpu.SMEM((3, NB), jnp.int32),
            pltpu.SMEM((3, TAPS), f32),
            pltpu.VMEM(observed.shape, f32),
            pltpu.VMEM(estimate.shape, f32),
            pltpu.SemaphoreType.DMA((6,)),
            pltpu.VMEM((256, 128), f32),
        ],
        compiler_params=pltpu.CompilerParams(collective_id=0, has_side_effects=True),
        name="splitting_step",
    )(slot_brick, neighbours.T, coords.T, blur_taps, observed, estimate)


def solution(mesh):
    split = P("bricks", "slab", None, None)
    return jax.shard_map(
        shards,
        mesh=mesh,
        in_specs=(split, split, P(), P(), P(), P()),
        out_specs=(split, split),
        check_vma=False,
    )
```

```python
import jax
import jax.numpy as jnp
from jax import lax
from jax.experimental import pallas as pl
from jax.experimental.pallas import tpu as pltpu
from jax.sharding import PartitionSpec as P

NB = 32
ND = 128
TAPS = 15
REACH = 7
SHRINK = 0.5
WEIGHT = 0.3
MESH = pl.DeviceIdType.MESH
f32 = jnp.float32
bf16 = jnp.bfloat16

EXCHANGES = {
    "est": (2, 2, "from"), "obs": (2, 2, "from"), "t1": (2, 2, ""), "t2": (2, 2, ""),
    "t3": (2, 2, ""), "t4": (2, 2, ""), "t5": (2, 2, ""), "t6": (2, 2, ""),
    "t7": (2, 2, "to"), "b0": (2, 2, "to"), "b1": (2, 2, "to"), "sums1": (1, 1, ""),
    "sums2": (1, 1, ""),
}
NAMES = list(EXCHANGES)


def kernel(slot_in, links_in, coords_in, taps_in, obs_in, est_in, sol_out, res_out, *scratch):
    n = len(NAMES)
    send = dict(zip(NAMES, scratch[:n]))
    recv = dict(zip(NAMES, scratch[n : 2 * n]))
    (fields, work, gathered, weights, turned_weights, blocks, planes0, planes1, planes2, smooth_sum,
     damp, source, peers, row_of, send_sems, recv_sems, plane_send, plane_recv, slot, links,
     coords, taps, obs_ref, est_ref, load_sems, partly, sol_ref, res_ref, store_sems) = scratch[2 * n :]
    planes = (planes0, planes1, planes2)
    ssem = {name: send_sems.at[k] for k, name in enumerate(NAMES)}
    rsem = {name: recv_sems.at[k] for k, name in enumerate(NAMES)}

    my_row = lax.axis_index("bricks")
    my_slab = lax.axis_index("slab")
    me = my_row // 2 * 8 + my_slab * 2 + lax.rem(my_row, 2)
    my_brick = my_row * 4 + my_slab
    my_z, my_y, my_core = my_row // 8, lax.rem(my_row // 2, 4), lax.rem(my_row, 2)
    slabs = [lax.rem(my_slab + d, 4) for d in range(4)]
    cores = [my_core, 1 - my_core]

    def far_first(j):
        return 2 + j - (j // 2) * (2 * j - 1)

    def everyone(visit):
        def group(step, carry):
            z = lax.rem(my_z + far_first(step // 4), 4)
            y = lax.rem(my_y + far_first(lax.rem(step, 4)), 4)
            for d in (2, 1, 3, 0):
                for c in (0, 1):
                    row = (z * 4 + y) * 2 + cores[c]
                    number = ((z * 4 + y) * 4 + slabs[d]) * 2 + cores[c]
                    visit(number, row * 4 + slabs[d], (row, slabs[d]))
            return carry

        lax.fori_loop(0, 15, group, 0)
        for d in (2, 1, 3, 0):
            for c in (1, 0):
                if d or c:
                    row = (my_z * 4 + my_y) * 2 + cores[c]
                    number = ((my_z * 4 + my_y) * 4 + slabs[d]) * 2 + cores[c]
                    visit(number, row * 4 + slabs[d], (row, slabs[d]))

    def start(name):
        rows, pitch, bricks = EXCHANGES[name]
        src, dst = send[name], recv[name]
        from_me = my_brick if bricks == "from" else me
        to_me = my_brick if bricks == "to" else me

        def part(ref, k):
            return ref.at[pl.ds(pl.multiple_of(pitch * k, pitch), rows)]

        def visit(number, place, device):
            pltpu.make_async_remote_copy(
                src_ref=part(src, place if bricks == "to" else number),
                dst_ref=part(dst, from_me), send_sem=ssem[name], recv_sem=rsem[name],
                device_id=device, device_id_type=MESH,
            ).start()

        everyone(visit)
        pltpu.make_async_copy(part(src, to_me), part(dst, from_me), rsem[name]).start()

    def arrive(name):
        dst = recv[name].at[pl.ds(0, ND * EXCHANGES[name][0])]
        pltpu.make_async_copy(dst, dst, rsem[name]).wait()

    barrier = pltpu.get_barrier_semaphore()

    def greet(number, place, device):
        pl.semaphore_signal(barrier, inc=1, device_id=device, device_id_type=MESH)

    everyone(greet)
    loads = [
        pltpu.make_async_copy(src, dst, load_sems.at[k])
        for k, (src, dst) in enumerate(
            ((est_in, est_ref), (obs_in, obs_ref), (slot_in, slot), (links_in, links),
             (coords_in, coords), (taps_in, taps)))
    ]
    for load in loads:
        load.start()
    for load in loads[:2]:
        load.wait()
    for h in range(2):
        block = est_ref[0, 8 * h : 8 * h + 8].reshape(128, 128)
        send["est"][pl.ds(h, 128, stride=2), :] = block.T
        send["obs"][pl.ds(h, 128, stride=2), :] = obs_ref[0, 8 * h : 8 * h + 8].reshape(128, 128)
    pl.semaphore_wait(barrier, ND - 1)
    start("est")
    start("obs")
    for load in loads[2:]:
        load.wait()

    zero = jnp.zeros((8, 128), f32)
    for ref in (fields.at[0], fields.at[1], fields.at[2], work,
                *(planes[op].at[side] for op in range(3) for side in range(2))):
        ref[NB] = zero

    def find_row(brick, carry):
        row = jnp.int32(0)
        for r in range(NB):
            row = jnp.where(slot[r] == brick, r, row)
        row_of[brick] = row
        return carry

    lax.fori_loop(0, NB, find_row, 0)

    def find_peers(row, carry):
        brick = slot[row]
        for k in range(6):
            link = links[k, brick]
            peers[row, k] = jnp.where(link >= 0, row_of[jnp.maximum(link, 0)], NB)
        return carry

    lax.fori_loop(0, NB, find_peers, 0)

    sub = lax.broadcasted_iota(jnp.int32, (8, 128), 0)
    lane = lax.broadcasted_iota(jnp.int32, (8, 128), 1)
    in_y = lax.rem(lane, 16)

    def make_weights(slot_at, axis, flipped, turned=False, keep=None):
        a = lax.broadcasted_iota(jnp.int32, (128, 128), 1 if turned else 0)
        b = lax.broadcasted_iota(jnp.int32, (128, 128), 0 if turned else 1)
        for side in range(3):
            if axis == 0:
                tap = 8 * (side - 1) + a // 16 - b // 16 + REACH
                fits = lax.rem(a, 16) == lax.rem(b, 16)
            elif axis == 1:
                tap = 16 * (side - 1) + lax.rem(a, 16) - lax.rem(b, 16) + REACH
                fits = a // 16 == b // 16
            else:
                tap = 128 * (side - 1) + a - b + REACH
                fits = a >= 0
            if flipped:
                tap = TAPS - 1 - tap
            tap = jnp.where(fits, tap, -1)

            def pick(t, total):
                return jnp.where(tap == t, taps[axis, t], total)

            block = lax.fori_loop(0, TAPS, pick, jnp.zeros((128, 128), f32))
            if keep is not None:
                blocks[keep, side] = block
            if turned and slot_at is not None:
                hold_turned(slot_at, side, block)
            elif slot_at is not None:
                high = block.astype(bf16)
                rows = pl.ds(128 * side, 128)
                weights[slot_at, rows, 0:128] = high
                weights[slot_at, rows, 128:256] = (block - high.astype(f32)).astype(bf16)

    def hold_turned(slot_at, at, block):
        high = block.astype(bf16)
        cols = pl.ds(128 * at, 128)
        turned_weights[slot_at, 0:128, cols] = high
        turned_weights[slot_at, 128:256, cols] = (block - high.astype(f32)).astype(bf16)

    def both_x_passes(slot_at):
        def through(back, forth):
            return jnp.dot(blocks[1, back], blocks[0, forth], precision=lax.Precision.HIGHEST,
                           preferred_element_type=f32)

        hold_turned(slot_at, 0, through(1, 0) + through(0, 1))
        hold_turned(slot_at, 1, through(1, 1))
        hold_turned(slot_at, 2, through(1, 2) + through(2, 1))
        hold_turned(slot_at, 3, through(0, 2) + through(2, 0))

    make_weights(0, 0, False)
    make_weights(0, 1, False, turned=True)

    def bricks_loop(body):
        def step(g, carry):
            for u in range(8):
                body(g * 8 + u)
            return carry

        lax.fori_loop(0, 4, step, 0)

    def gather(ref, axis, ends=False):
        for b in range(NB):
            own = ref[b]
            lower = ref[peers[b, 2 * axis]]
            upper = ref[peers[b, 2 * axis + 1]]
            if axis == 0:
                lower = pltpu.roll(jnp.where(sub == 7, lower, own), 1, 0)
                upper = pltpu.roll(jnp.where(sub == 0, upper, own), 7, 0)
            gathered[b, :, 0:128] = lower
            gathered[b, :, 128:256] = own
            gathered[b, :, 256:384] = upper
            if ends:
                has_lower = jnp.where(peers[b, 4] < NB, 1.0, 0.0)
                has_upper = jnp.where(peers[b, 5] < NB, 1.0, 0.0)
                inner = jnp.where(lane >= 128 - REACH, own * has_upper, 0.0)
                gathered[b, :, 384:512] = jnp.where(lane < REACH, own * has_lower, inner)

    def split(values):
        high = values.astype(bf16)
        return high, (values - high.astype(f32)).astype(bf16)

    def operands(ref, axis, ends):
        gather(ref, axis, ends)
        depth = 512 if ends else 384
        return depth, *split(gathered[:, :, 0:depth].reshape(256, depth))

    def dot(a, b, contract):
        return lax.dot_general(a, b, (contract, ((), ())), preferred_element_type=f32)

    def apply(ref, axis, which):
        _, high, low = operands(ref, axis, False)
        both = dot(high, weights[which], ((1,), (0,)))
        rest = dot(low, weights[which, :, 0:128], ((1,), (0,)))
        return both[:, 0:128] + both[:, 128:256] + rest

    def apply_turned(ref, axis, which, ends=False):
        depth, high, low = operands(ref, axis, ends)
        both = dot(turned_weights[which, :, 0:depth], high, ((1,), (1,)))
        rest = dot(turned_weights[which, 0:128, 0:depth], low, ((1,), (1,)))
        return both[0:128] + both[128:256] + rest

    def post(name, turned):
        rows = EXCHANGES[name][1]
        for h in range(2):
            send[name][pl.ds(h, 128, stride=rows), :] = turned[:, 128 * h : 128 * h + 128]

    def unpack(name, ref, scale=None):
        rows = EXCHANGES[name][1]
        for h in range(2):
            block = recv[name][pl.ds(h, 128, stride=rows), :].T
            block = block.reshape(16, 8, 128)
            if scale is not None:
                block = block * scale[16 * h : 16 * h + 16]
            ref[16 * h : 16 * h + 16] = block

    def plane_copies(op):
        copies = []
        for side, shift in ((0, 1), (1, ND - 1)):
            other = lax.rem(me + shift, ND)
            chip, core = other // 2, lax.rem(other, 2)
            copies.append(
                pltpu.make_async_remote_copy(
                    src_ref=fields.at[op, pl.ds(0, NB)],
                    dst_ref=planes[op].at[side, pl.ds(0, NB)],
                    send_sem=plane_send.at[op, side], recv_sem=plane_recv.at[op, side],
                    device_id=(chip // 4 * 2 + core, lax.rem(chip, 4)),
                    device_id_type=MESH,
                )
            )
        return copies

    def around(op, b):
        field = fields.at[op]
        own = field[b]
        z_low, z_high, y_low, y_high = (field[peers[b, k]] for k in range(4))
        down = pltpu.roll(jnp.where(sub == 7, z_low, own), 1, 0)
        up = pltpu.roll(jnp.where(sub == 0, z_high, own), 7, 0)
        before_z = pltpu.roll(jnp.where(lane >= 112, down, own), 16, 1)
        beyond_z = pltpu.roll(jnp.where(lane < 16, up, own), 112, 1)
        before_y = pltpu.roll(jnp.where(in_y == 15, pltpu.roll(y_low, 112, 1), own), 1, 1)
        beyond_y = pltpu.roll(jnp.where(in_y == 0, pltpu.roll(y_high, 16, 1), own), 127, 1)
        before_x = planes[op][0, jnp.where(me == 0, peers[b, 4], b)]
        beyond_x = planes[op][1, jnp.where(me == ND - 1, peers[b, 5], b)]
        has = [jnp.where(peers[b, 2 * k] < NB, 1.0, 0.0) for k in range(3)]
        low_z = jnp.where((sub == 0) & (lane < 16), has[0], 1.0)
        low_y = jnp.where(in_y == 0, has[1], 1.0)
        low_x = jnp.where(me == 0, has[2], 1.0)
        return own, ((before_z, beyond_z, low_z), (before_y, beyond_y, low_y),
                     (before_x, beyond_x, low_x))

    def smooth_shrunk(op):
        def penalty(g):
            return -SHRINK * g / (g * g + SHRINK)

        def body(b):
            own, sides = around(op, b)
            total = zero
            for before, beyond, low in sides:
                total = total + penalty(own - before) * low - penalty(beyond - own)
            smooth_sum[op, b] = WEIGHT * total

        bricks_loop(body)

    def smooth_linear(op):
        def body(b):
            own, sides = around(op, b)
            total = zero
            for before, beyond, low in sides:
                total = total + (own - before) * low - (beyond - own)
            smooth_sum[op, b] = WEIGHT * total

        bricks_loop(body)

    def operate(op, to_zy, to_x, first, before_x=None, meanwhile=None):
        planes_moving = plane_copies(op)
        work[0:NB] = apply(fields.at[op], 0, 0).reshape(NB, 8, 128)
        post(to_zy, apply_turned(work, 1, 0))
        start(to_zy)
        for copy in planes_moving:
            copy.start()
        if before_x is not None:
            before_x()
        arrive(to_zy)
        unpack(to_zy, work, damp)
        turned = apply_turned(work, 2, 1, ends=True)
        post(to_x, source[...] - turned if first else turned)
        start(to_x)
        for copy in planes_moving:
            copy.wait()
        if first:
            smooth_shrunk(op)
        else:
            smooth_linear(op)
        if meanwhile is not None:
            meanwhile()
        arrive(to_x)
        unpack(to_x, work)
        work[0:NB] = apply(work, 1, 1).reshape(NB, 8, 128)
        return apply(work, 0, 2).reshape(NB, 8, 128) + smooth_sum[op]

    arrive("est")
    fields[0, 0:NB] = recv["est"][...].reshape(NB, 8, 128)

    def prepare():
        make_weights(None, 2, False, turned=True, keep=0)
        make_weights(2, 2, True, turned=True, keep=1)
        both_x_passes(1)

        def body(b):
            depth = coords[0, slot[b]] * 64 + 8 * sub + me // 16
            damp[b] = jnp.exp(-depth.astype(f32) / 256.0)

        bricks_loop(body)
        arrive("obs")
        work[0:NB] = damp[...] * recv["obs"][...].reshape(NB, 8, 128)
        source[...] = apply_turned(work, 2, 2)
        damp[...] = damp[...] * damp[...]

    def prepare_adjoint():
        make_weights(1, 1, True)
        make_weights(2, 0, True)

    fields[1, 0:NB] = operate(0, "t1", "t2", True, before_x=prepare, meanwhile=prepare_adjoint)

    def send_r0():
        send["b0"][...] = fields[1, 0:NB].reshape(256, 128)
        start("b0")

    fields[2, 0:NB] = operate(1, "t3", "t4", False, before_x=send_r0)

    low_half = lax.broadcasted_iota(jnp.int32, (1, 128), 1) < 64

    def two_sums(first, second):
        a = jnp.sum(first, axis=0, keepdims=True)
        b = jnp.sum(second, axis=0, keepdims=True)
        a = a + pltpu.roll(a, 64, 1)
        b = b + pltpu.roll(b, 64, 1)
        return jnp.where(low_half, a, b)

    def send_w1():
        r0, w1 = fields[1, 0:NB].reshape(256, 128), fields[2, 0:NB].reshape(256, 128)
        send["sums1"][...] = jnp.broadcast_to(two_sums(r0 * r0, r0 * w1), (128, 128))
        start("sums1")
        send["b1"][...] = w1
        start("b1")

    def total_of(rows):
        return jnp.sum(rows, keepdims=True)

    lane_of = lax.broadcasted_iota(jnp.int32, (128, 128), 1)

    def first_step():
        arrive("sums1")
        rr = total_of(jnp.where(lane_of < 64, recv["sums1"][...], 0.0))
        r0w1 = total_of(jnp.where(lane_of < 64, 0.0, recv["sums1"][...]))
        return rr, r0w1, rr / r0w1

    def send_sums():
        rr, r0w1, step1 = first_step()
        r0, w1 = fields[1, 0:NB].reshape(256, 128), fields[2, 0:NB].reshape(256, 128)
        r1 = r0 - step1 * w1
        smooth1 = (smooth_sum[1] - step1 * smooth_sum[2]).reshape(256, 128)
        blurred = recv["t3"][...] - step1 * recv["t5"][...]
        passed = send["t4"][...] - step1 * send["t6"][...]
        first_pair = two_sums(r1 * r1, r1 * smooth1 + blurred * passed)
        second = jnp.sum(r1 * w1, axis=0, keepdims=True)
        for shift in (64, 32):
            second = second + pltpu.roll(second, shift, 1)
        first_pair = first_pair + pltpu.roll(first_pair, 96, 1)
        quarter = lax.rem(lax.broadcasted_iota(jnp.int32, (1, 128), 1), 64) < 32
        send["sums2"][...] = jnp.broadcast_to(jnp.where(quarter, first_pair, second), (128, 128))
        start("sums2")
        steps.extend((rr, r0w1, step1))

    steps = []
    work_out = operate(2, "t5", "t6", False, before_x=send_w1, meanwhile=send_sums)
    send["t7"][...] = work_out.reshape(256, 128)
    start("t7")
    rr, r0w1, step1 = steps
    arrive("b0")
    arrive("b1")
    arrive("sums2")
    sums = recv["sums2"][...]
    inner = lax.rem(lane_of, 64) < 32
    rr1 = total_of(jnp.where(inner & (lane_of < 64), sums, 0.0))
    r1ar1 = total_of(jnp.where(inner & (lane_of >= 64), sums, 0.0))
    r1w1 = total_of(jnp.where(lane_of < 64, jnp.where(inner, 0.0, sums), 0.0))
    ratio = rr1 / rr
    step2 = rr1 / (r1ar1 + 2.0 * ratio * r1w1 + ratio * ratio * r0w1)
    for h in range(2):
        b0 = recv["b0"][pl.ds(h, 128, stride=2), :].T
        b1 = recv["b1"][pl.ds(h, 128, stride=2), :].T
        r = b0 - step1 * b1
        est = est_ref[0, 8 * h : 8 * h + 8].reshape(128, 128)
        sol = est + step1 * b0 + step2 * (r + ratio * b0)
        sol_ref[0, 8 * h : 8 * h + 8] = sol.reshape(8, 16, 128)
        partly[128 * h : 128 * h + 128] = r - step2 * (b1 + ratio * b1)
    stores = [pltpu.make_async_copy(sol_ref, sol_out, store_sems.at[0])]
    stores[0].start()
    arrive("t7")
    for h in range(2):
        b2 = recv["t7"][pl.ds(h, 128, stride=2), :].T
        res = partly[128 * h : 128 * h + 128] + step2 * step1 * b2
        res_ref[0, 8 * h : 8 * h + 8] = res.reshape(8, 16, 128)
        half = pl.ds(8 * h, 8)
        stores.append(
            pltpu.make_async_copy(res_ref.at[:, half], res_out.at[:, half], store_sems.at[1 + h]))
        stores[-1].start()

    for store in stores:
        store.wait()
    for name in NAMES:
        sent = send[name].at[pl.ds(0, (ND - 1) * EXCHANGES[name][0])]
        pltpu.make_async_copy(sent, sent, ssem[name]).wait()


def hand_over(sol_in, res_in, sol_out, res_out, held, load_sems, store_sems):
    loads, stores = [], []
    for k, (src, dst) in enumerate(((sol_in, sol_out), (res_in, res_out))):
        for h in range(2):
            half = pl.ds(8 * h, 8)
            here = held.at[k, :, half]
            loads.append(pltpu.make_async_copy(src.at[:, half], here, load_sems.at[2 * k + h]))
            stores.append(pltpu.make_async_copy(here, dst.at[:, half], store_sems.at[2 * k + h]))
            loads[-1].start()
    for load, store in zip(loads, stores):
        load.wait()
        store.start()
    for store in stores:
        store.wait()


def shards(observed, estimate, blur_taps, slot_brick, neighbours, coords):
    place = pl.BlockSpec(memory_space=pl.ANY)
    shape = jax.ShapeDtypeStruct(estimate.shape, f32)
    buffers = [pltpu.VMEM((ND * EXCHANGES[name][1], 128), f32) for name in NAMES]
    count = len(NAMES)
    found = pl.pallas_call(
        kernel,
        out_shape=(shape, shape),
        in_specs=[place] * 6,
        out_specs=(place, place),
        scratch_shapes=buffers + buffers + [
            pltpu.VMEM((3, NB + 1, 8, 128), f32),
            pltpu.VMEM((NB + 1, 8, 128), f32),
            pltpu.VMEM((NB, 8, 512), f32),
            pltpu.VMEM((3, 384, 256), bf16),
            pltpu.VMEM((3, 256, 512), bf16),
            pltpu.VMEM((2, 3, 128, 128), f32),
            *[pltpu.VMEM((2, NB + 1, 8, 128), f32)] * 3,
            pltpu.VMEM((3, NB, 8, 128), f32),
            pltpu.VMEM((NB, 8, 128), f32),
            pltpu.VMEM((128, 256), f32),
            pltpu.SMEM((NB, 6), jnp.int32),
            pltpu.SMEM((NB,), jnp.int32),
            pltpu.SemaphoreType.DMA((count,)),
            pltpu.SemaphoreType.DMA((count,)),
            pltpu.SemaphoreType.DMA((3, 2)),
            pltpu.SemaphoreType.DMA((3, 2)),
            pltpu.SMEM((NB,), jnp.int32),
            pltpu.SMEM((6, NB), jnp.int32),
            pltpu.SMEM((3, NB), jnp.int32),
            pltpu.SMEM((3, TAPS), f32),
            pltpu.VMEM(observed.shape, f32),
            pltpu.VMEM(estimate.shape, f32),
            pltpu.SemaphoreType.DMA((6,)),
            pltpu.VMEM((256, 128), f32),
            pltpu.VMEM(estimate.shape, f32),
            pltpu.VMEM(estimate.shape, f32),
            pltpu.SemaphoreType.DMA((3,)),
        ],
        compiler_params=pltpu.CompilerParams(collective_id=0, has_side_effects=True),
        name="splitting_step",
    )(slot_brick, neighbours.T, coords.T, blur_taps, observed, estimate)
    return pl.pallas_call(
        hand_over,
        out_shape=(shape, shape),
        in_specs=[place] * 2,
        out_specs=(place, place),
        scratch_shapes=[
            pltpu.VMEM((2, *estimate.shape), f32),
            pltpu.SemaphoreType.DMA((4,)),
            pltpu.SemaphoreType.DMA((4,)),
        ],
        name="hand_over",
    )(*found)


def solution(mesh):
    split = P("bricks", "slab", None, None)
    return jax.shard_map(
        shards,
        mesh=mesh,
        in_specs=(split, split, P(), P(), P(), P()),
        out_specs=(split, split),
        check_vma=False,
    )
```

```python
import jax
import jax.numpy as jnp
from jax import lax
from jax.experimental import pallas as pl
from jax.experimental.pallas import tpu as pltpu
from jax.sharding import PartitionSpec as P

NB = 32
ND = 128
TAPS = 15
REACH = 7
SHRINK = 0.5
WEIGHT = 0.3
MESH = pl.DeviceIdType.MESH
f32 = jnp.float32
bf16 = jnp.bfloat16

EXCHANGES = {
    "est": (2, 2, "from"), "obs": (2, 2, "from"), "t1": (2, 2, ""), "t2": (2, 2, ""),
    "t3": (2, 2, ""), "t4": (2, 2, ""), "t5": (2, 2, ""), "t6": (2, 2, ""),
    "t7": (2, 2, "to"), "b0": (2, 2, "to"), "b1": (2, 2, "to"), "sums1": (1, 1, ""),
    "sums2": (1, 1, ""),
}
NAMES = list(EXCHANGES)


def kernel(slot_in, links_in, coords_in, taps_in, obs_in, est_in, sol_out, res_out, *scratch):
    n = len(NAMES)
    send = dict(zip(NAMES, scratch[:n]))
    recv = dict(zip(NAMES, scratch[n : 2 * n]))
    (fields, work, gathered, weights, turned_weights, blocks, planes0, planes1, planes2, smooth_sum,
     damp, source, peers, row_of, send_sems, recv_sems, plane_send, plane_recv, slot, links,
     coords, taps, obs_ref, est_ref, load_sems, partly, sol_ref, res_ref, store_sems) = scratch[2 * n :]
    planes = (planes0, planes1, planes2)
    ssem = {name: send_sems.at[k] for k, name in enumerate(NAMES)}
    rsem = {name: recv_sems.at[k] for k, name in enumerate(NAMES)}

    my_row = lax.axis_index("bricks")
    my_slab = lax.axis_index("slab")
    me = my_row // 2 * 8 + my_slab * 2 + lax.rem(my_row, 2)
    my_brick = my_row * 4 + my_slab
    my_z, my_y, my_core = my_row // 8, lax.rem(my_row // 2, 4), lax.rem(my_row, 2)
    slabs = [lax.rem(my_slab + d, 4) for d in range(4)]
    cores = [my_core, 1 - my_core]

    def far_first(j):
        return 2 + j - (j // 2) * (2 * j - 1)

    def everyone(visit):
        def group(step, carry):
            z = lax.rem(my_z + far_first(step // 4), 4)
            y = lax.rem(my_y + far_first(lax.rem(step, 4)), 4)
            for d in (2, 1, 3, 0):
                for c in (0, 1):
                    row = (z * 4 + y) * 2 + cores[c]
                    number = ((z * 4 + y) * 4 + slabs[d]) * 2 + cores[c]
                    visit(number, row * 4 + slabs[d], (row, slabs[d]))
            return carry

        lax.fori_loop(0, 15, group, 0)
        for d in (2, 1, 3, 0):
            for c in (1, 0):
                if d or c:
                    row = (my_z * 4 + my_y) * 2 + cores[c]
                    number = ((my_z * 4 + my_y) * 4 + slabs[d]) * 2 + cores[c]
                    visit(number, row * 4 + slabs[d], (row, slabs[d]))

    def start(name):
        rows, pitch, bricks = EXCHANGES[name]
        src, dst = send[name], recv[name]
        from_me = my_brick if bricks == "from" else me
        to_me = my_brick if bricks == "to" else me

        def part(ref, k):
            return ref.at[pl.ds(pl.multiple_of(pitch * k, pitch), rows)]

        def visit(number, place, device):
            pltpu.make_async_remote_copy(
                src_ref=part(src, place if bricks == "to" else number),
                dst_ref=part(dst, from_me), send_sem=ssem[name], recv_sem=rsem[name],
                device_id=device, device_id_type=MESH,
            ).start()

        everyone(visit)
        pltpu.make_async_copy(part(src, to_me), part(dst, from_me), rsem[name]).start()

    def arrive(name):
        dst = recv[name].at[pl.ds(0, ND * EXCHANGES[name][0])]
        pltpu.make_async_copy(dst, dst, rsem[name]).wait()

    barrier = pltpu.get_barrier_semaphore()

    def greet(number, place, device):
        pl.semaphore_signal(barrier, inc=1, device_id=device, device_id_type=MESH)

    everyone(greet)
    loads = [
        pltpu.make_async_copy(src, dst, load_sems.at[k])
        for k, (src, dst) in enumerate(
            ((est_in, est_ref), (obs_in, obs_ref), (slot_in, slot), (links_in, links),
             (coords_in, coords), (taps_in, taps)))
    ]
    for load in loads:
        load.start()
    for load in loads[:2]:
        load.wait()
    for h in range(2):
        block = est_ref[0, 8 * h : 8 * h + 8].reshape(128, 128)
        send["est"][pl.ds(h, 128, stride=2), :] = block.T
        send["obs"][pl.ds(h, 128, stride=2), :] = obs_ref[0, 8 * h : 8 * h + 8].reshape(128, 128)
    pl.semaphore_wait(barrier, ND - 1)
    start("est")
    start("obs")
    for load in loads[2:]:
        load.wait()

    zero = jnp.zeros((8, 128), f32)
    for ref in (fields.at[0], fields.at[1], fields.at[2], work,
                *(planes[op].at[side] for op in range(3) for side in range(2))):
        ref[NB] = zero

    def find_row(brick, carry):
        row = jnp.int32(0)
        for r in range(NB):
            row = jnp.where(slot[r] == brick, r, row)
        row_of[brick] = row
        return carry

    lax.fori_loop(0, NB, find_row, 0)

    def find_peers(row, carry):
        brick = slot[row]
        for k in range(6):
            link = links[k, brick]
            peers[row, k] = jnp.where(link >= 0, row_of[jnp.maximum(link, 0)], NB)
        return carry

    lax.fori_loop(0, NB, find_peers, 0)

    sub = lax.broadcasted_iota(jnp.int32, (8, 128), 0)
    lane = lax.broadcasted_iota(jnp.int32, (8, 128), 1)
    in_y = lax.rem(lane, 16)

    def make_weights(slot_at, axis, flipped, turned=False, keep=None):
        a = lax.broadcasted_iota(jnp.int32, (128, 128), 1 if turned else 0)
        b = lax.broadcasted_iota(jnp.int32, (128, 128), 0 if turned else 1)
        for side in range(3):
            if axis == 0:
                tap = 8 * (side - 1) + a // 16 - b // 16 + REACH
                fits = lax.rem(a, 16) == lax.rem(b, 16)
            elif axis == 1:
                tap = 16 * (side - 1) + lax.rem(a, 16) - lax.rem(b, 16) + REACH
                fits = a // 16 == b // 16
            else:
                tap = 128 * (side - 1) + a - b + REACH
                fits = a >= 0
            if flipped:
                tap = TAPS - 1 - tap
            tap = jnp.where(fits, tap, -1)

            def pick(t, total):
                return jnp.where(tap == t, taps[axis, t], total)

            block = lax.fori_loop(0, TAPS, pick, jnp.zeros((128, 128), f32))
            if keep is not None:
                blocks[keep, side] = block
            if turned and slot_at is not None:
                hold_turned(slot_at, side, block)
            elif slot_at is not None:
                high = block.astype(bf16)
                rows = pl.ds(128 * side, 128)
                weights[slot_at, rows, 0:128] = high
                weights[slot_at, rows, 128:256] = (block - high.astype(f32)).astype(bf16)

    def hold_turned(slot_at, at, block):
        high = block.astype(bf16)
        cols = pl.ds(128 * at, 128)
        turned_weights[slot_at, 0:128, cols] = high
        turned_weights[slot_at, 128:256, cols] = (block - high.astype(f32)).astype(bf16)

    def both_x_passes(slot_at):
        def through(back, forth):
            return jnp.dot(blocks[1, back], blocks[0, forth], precision=lax.Precision.HIGHEST,
                           preferred_element_type=f32)

        hold_turned(slot_at, 0, through(1, 0) + through(0, 1))
        hold_turned(slot_at, 1, through(1, 1))
        hold_turned(slot_at, 2, through(1, 2) + through(2, 1))
        hold_turned(slot_at, 3, through(0, 2) + through(2, 0))

    make_weights(0, 0, False)
    make_weights(0, 1, False, turned=True)

    def bricks_loop(body):
        def step(g, carry):
            for u in range(8):
                body(g * 8 + u)
            return carry

        lax.fori_loop(0, 4, step, 0)

    def gather(ref, axis, ends=False):
        for b in range(NB):
            own = ref[b]
            lower = ref[peers[b, 2 * axis]]
            upper = ref[peers[b, 2 * axis + 1]]
            if axis == 0:
                lower = pltpu.roll(jnp.where(sub == 7, lower, own), 1, 0)
                upper = pltpu.roll(jnp.where(sub == 0, upper, own), 7, 0)
            gathered[b, :, 0:128] = lower
            gathered[b, :, 128:256] = own
            gathered[b, :, 256:384] = upper
            if ends:
                has_lower = jnp.where(peers[b, 4] < NB, 1.0, 0.0)
                has_upper = jnp.where(peers[b, 5] < NB, 1.0, 0.0)
                inner = jnp.where(lane >= 128 - REACH, own * has_upper, 0.0)
                gathered[b, :, 384:512] = jnp.where(lane < REACH, own * has_lower, inner)

    def split(values):
        high = values.astype(bf16)
        return high, (values - high.astype(f32)).astype(bf16)

    def operands(ref, axis, ends):
        gather(ref, axis, ends)
        depth = 512 if ends else 384
        return depth, *split(gathered[:, :, 0:depth].reshape(256, depth))

    def dot(a, b, contract):
        return lax.dot_general(a, b, (contract, ((), ())), preferred_element_type=f32)

    def apply(ref, axis, which):
        _, high, low = operands(ref, axis, False)
        both = dot(high, weights[which], ((1,), (0,)))
        rest = dot(low, weights[which, :, 0:128], ((1,), (0,)))
        return both[:, 0:128] + both[:, 128:256] + rest

    def apply_turned(ref, axis, which, ends=False):
        depth, high, low = operands(ref, axis, ends)
        both = dot(turned_weights[which, :, 0:depth], high, ((1,), (1,)))
        rest = dot(turned_weights[which, 0:128, 0:depth], low, ((1,), (1,)))
        return both[0:128] + both[128:256] + rest

    def post(name, turned):
        rows = EXCHANGES[name][1]
        for h in range(2):
            send[name][pl.ds(h, 128, stride=rows), :] = turned[:, 128 * h : 128 * h + 128]

    def unpack(name, ref, scale=None):
        rows = EXCHANGES[name][1]
        for h in range(2):
            block = recv[name][pl.ds(h, 128, stride=rows), :].T
            block = block.reshape(16, 8, 128)
            if scale is not None:
                block = block * scale[16 * h : 16 * h + 16]
            ref[16 * h : 16 * h + 16] = block

    def plane_copies(op):
        copies = []
        for side, shift in ((0, 1), (1, ND - 1)):
            other = lax.rem(me + shift, ND)
            chip, core = other // 2, lax.rem(other, 2)
            copies.append(
                pltpu.make_async_remote_copy(
                    src_ref=fields.at[op, pl.ds(0, NB)],
                    dst_ref=planes[op].at[side, pl.ds(0, NB)],
                    send_sem=plane_send.at[op, side], recv_sem=plane_recv.at[op, side],
                    device_id=(chip // 4 * 2 + core, lax.rem(chip, 4)),
                    device_id_type=MESH,
                )
            )
        return copies

    def around(op, b):
        field = fields.at[op]
        own = field[b]
        z_low, z_high, y_low, y_high = (field[peers[b, k]] for k in range(4))
        down = pltpu.roll(jnp.where(sub == 7, z_low, own), 1, 0)
        up = pltpu.roll(jnp.where(sub == 0, z_high, own), 7, 0)
        before_z = pltpu.roll(jnp.where(lane >= 112, down, own), 16, 1)
        beyond_z = pltpu.roll(jnp.where(lane < 16, up, own), 112, 1)
        before_y = pltpu.roll(jnp.where(in_y == 15, pltpu.roll(y_low, 112, 1), own), 1, 1)
        beyond_y = pltpu.roll(jnp.where(in_y == 0, pltpu.roll(y_high, 16, 1), own), 127, 1)
        before_x = planes[op][0, jnp.where(me == 0, peers[b, 4], b)]
        beyond_x = planes[op][1, jnp.where(me == ND - 1, peers[b, 5], b)]
        has = [jnp.where(peers[b, 2 * k] < NB, 1.0, 0.0) for k in range(3)]
        low_z = jnp.where((sub == 0) & (lane < 16), has[0], 1.0)
        low_y = jnp.where(in_y == 0, has[1], 1.0)
        low_x = jnp.where(me == 0, has[2], 1.0)
        return own, ((before_z, beyond_z, low_z), (before_y, beyond_y, low_y),
                     (before_x, beyond_x, low_x))

    def smooth_shrunk(op):
        def penalty(g):
            return -SHRINK * g / (g * g + SHRINK)

        def body(b):
            own, sides = around(op, b)
            total = zero
            for before, beyond, low in sides:
                total = total + penalty(own - before) * low - penalty(beyond - own)
            smooth_sum[op, b] = WEIGHT * total

        bricks_loop(body)

    def smooth_linear(op):
        def body(b):
            own, sides = around(op, b)
            total = zero
            for before, beyond, low in sides:
                total = total + (own - before) * low - (beyond - own)
            smooth_sum[op, b] = WEIGHT * total

        bricks_loop(body)

    def operate(op, to_zy, to_x, first, before_x=None, meanwhile=None):
        planes_moving = plane_copies(op)
        work[0:NB] = apply(fields.at[op], 0, 0).reshape(NB, 8, 128)
        post(to_zy, apply_turned(work, 1, 0))
        start(to_zy)
        for copy in planes_moving:
            copy.start()
        if before_x is not None:
            before_x()
        arrive(to_zy)
        unpack(to_zy, work, damp)
        turned = apply_turned(work, 2, 1, ends=True)
        post(to_x, source[...] - turned if first else turned)
        start(to_x)
        for copy in planes_moving:
            copy.wait()
        if first:
            smooth_shrunk(op)
        else:
            smooth_linear(op)
        if meanwhile is not None:
            meanwhile()
        arrive(to_x)
        unpack(to_x, work)
        work[0:NB] = apply(work, 1, 1).reshape(NB, 8, 128)
        return apply(work, 0, 2).reshape(NB, 8, 128) + smooth_sum[op]

    arrive("est")
    fields[0, 0:NB] = recv["est"][...].reshape(NB, 8, 128)

    def prepare():
        make_weights(None, 2, False, turned=True, keep=0)
        make_weights(2, 2, True, turned=True, keep=1)
        both_x_passes(1)

        def body(b):
            depth = coords[0, slot[b]] * 64 + 8 * sub + me // 16
            damp[b] = jnp.exp(-depth.astype(f32) / 256.0)

        bricks_loop(body)
        arrive("obs")
        work[0:NB] = damp[...] * recv["obs"][...].reshape(NB, 8, 128)
        source[...] = apply_turned(work, 2, 2)
        damp[...] = damp[...] * damp[...]

    def prepare_adjoint():
        make_weights(1, 1, True)
        make_weights(2, 0, True)

    fields[1, 0:NB] = operate(0, "t1", "t2", True, before_x=prepare, meanwhile=prepare_adjoint)

    def send_r0():
        send["b0"][...] = fields[1, 0:NB].reshape(256, 128)
        start("b0")

    fields[2, 0:NB] = operate(1, "t3", "t4", False, before_x=send_r0)

    low_half = lax.broadcasted_iota(jnp.int32, (1, 128), 1) < 64

    def two_sums(first, second):
        a = jnp.sum(first, axis=0, keepdims=True)
        b = jnp.sum(second, axis=0, keepdims=True)
        a = a + pltpu.roll(a, 64, 1)
        b = b + pltpu.roll(b, 64, 1)
        return jnp.where(low_half, a, b)

    def send_w1():
        r0, w1 = fields[1, 0:NB].reshape(256, 128), fields[2, 0:NB].reshape(256, 128)
        send["sums1"][...] = jnp.broadcast_to(two_sums(r0 * r0, r0 * w1), (128, 128))
        start("sums1")
        send["b1"][...] = w1
        start("b1")

    def total_of(rows):
        return jnp.sum(rows, keepdims=True)

    lane_of = lax.broadcasted_iota(jnp.int32, (128, 128), 1)

    def first_step():
        arrive("sums1")
        rr = total_of(jnp.where(lane_of < 64, recv["sums1"][...], 0.0))
        r0w1 = total_of(jnp.where(lane_of < 64, 0.0, recv["sums1"][...]))
        return rr, r0w1, rr / r0w1

    def send_sums():
        rr, r0w1, step1 = first_step()
        r0, w1 = fields[1, 0:NB].reshape(256, 128), fields[2, 0:NB].reshape(256, 128)
        r1 = r0 - step1 * w1
        smooth1 = (smooth_sum[1] - step1 * smooth_sum[2]).reshape(256, 128)
        blurred = recv["t3"][...] - step1 * recv["t5"][...]
        passed = send["t4"][...] - step1 * send["t6"][...]
        first_pair = two_sums(r1 * r1, r1 * smooth1 + blurred * passed)
        second = jnp.sum(r1 * w1, axis=0, keepdims=True)
        for shift in (64, 32):
            second = second + pltpu.roll(second, shift, 1)
        first_pair = first_pair + pltpu.roll(first_pair, 96, 1)
        quarter = lax.rem(lax.broadcasted_iota(jnp.int32, (1, 128), 1), 64) < 32
        send["sums2"][...] = jnp.broadcast_to(jnp.where(quarter, first_pair, second), (128, 128))
        start("sums2")
        steps.extend((rr, r0w1, step1))

    steps = []
    work_out = operate(2, "t5", "t6", False, before_x=send_w1, meanwhile=send_sums)
    send["t7"][...] = work_out.reshape(256, 128)
    start("t7")
    rr, r0w1, step1 = steps
    arrive("b0")
    arrive("b1")
    arrive("sums2")
    sums = recv["sums2"][...]
    inner = lax.rem(lane_of, 64) < 32
    rr1 = total_of(jnp.where(inner & (lane_of < 64), sums, 0.0))
    r1ar1 = total_of(jnp.where(inner & (lane_of >= 64), sums, 0.0))
    r1w1 = total_of(jnp.where(lane_of < 64, jnp.where(inner, 0.0, sums), 0.0))
    ratio = rr1 / rr
    step2 = rr1 / (r1ar1 + 2.0 * ratio * r1w1 + ratio * ratio * r0w1)
    for h in range(2):
        b0 = recv["b0"][pl.ds(h, 128, stride=2), :].T
        b1 = recv["b1"][pl.ds(h, 128, stride=2), :].T
        r = b0 - step1 * b1
        est = est_ref[0, 8 * h : 8 * h + 8].reshape(128, 128)
        sol = est + step1 * b0 + step2 * (r + ratio * b0)
        sol_ref[0, 8 * h : 8 * h + 8] = sol.reshape(8, 16, 128)
        partly[128 * h : 128 * h + 128] = r - step2 * (b1 + ratio * b1)
    stores = [pltpu.make_async_copy(sol_ref, sol_out, store_sems.at[0])]
    stores[0].start()
    arrive("t7")
    for h in range(2):
        b2 = recv["t7"][pl.ds(h, 128, stride=2), :].T
        res = partly[128 * h : 128 * h + 128] + step2 * step1 * b2
        res_ref[0, 8 * h : 8 * h + 8] = res.reshape(8, 16, 128)
        half = pl.ds(8 * h, 8)
        stores.append(
            pltpu.make_async_copy(res_ref.at[:, half], res_out.at[:, half], store_sems.at[1 + h]))
        stores[-1].start()

    for store in stores:
        store.wait()
    for name in NAMES:
        sent = send[name].at[pl.ds(0, (ND - 1) * EXCHANGES[name][0])]
        pltpu.make_async_copy(sent, sent, ssem[name]).wait()


def hand_over(sol_in, res_in, sol_out, res_out, held, load_sems, store_sems):
    loads, stores = [], []
    for k, (src, dst) in enumerate(((sol_in, sol_out), (res_in, res_out))):
        for h in range(4):
            half = pl.ds(4 * h, 4)
            here = held.at[k, :, half]
            loads.append(pltpu.make_async_copy(src.at[:, half], here, load_sems.at[4 * k + h]))
            stores.append(pltpu.make_async_copy(here, dst.at[:, half], store_sems.at[4 * k + h]))
            loads[-1].start()
    for load, store in zip(loads, stores):
        load.wait()
        store.start()
    for store in stores:
        store.wait()


def shards(observed, estimate, blur_taps, slot_brick, neighbours, coords):
    place = pl.BlockSpec(memory_space=pl.ANY)
    shape = jax.ShapeDtypeStruct(estimate.shape, f32)
    buffers = [pltpu.VMEM((ND * EXCHANGES[name][1], 128), f32) for name in NAMES]
    count = len(NAMES)
    found = pl.pallas_call(
        kernel,
        out_shape=(shape, shape),
        in_specs=[place] * 6,
        out_specs=(place, place),
        scratch_shapes=buffers + buffers + [
            pltpu.VMEM((3, NB + 1, 8, 128), f32),
            pltpu.VMEM((NB + 1, 8, 128), f32),
            pltpu.VMEM((NB, 8, 512), f32),
            pltpu.VMEM((3, 384, 256), bf16),
            pltpu.VMEM((3, 256, 512), bf16),
            pltpu.VMEM((2, 3, 128, 128), f32),
            *[pltpu.VMEM((2, NB + 1, 8, 128), f32)] * 3,
            pltpu.VMEM((3, NB, 8, 128), f32),
            pltpu.VMEM((NB, 8, 128), f32),
            pltpu.VMEM((128, 256), f32),
            pltpu.SMEM((NB, 6), jnp.int32),
            pltpu.SMEM((NB,), jnp.int32),
            pltpu.SemaphoreType.DMA((count,)),
            pltpu.SemaphoreType.DMA((count,)),
            pltpu.SemaphoreType.DMA((3, 2)),
            pltpu.SemaphoreType.DMA((3, 2)),
            pltpu.SMEM((NB,), jnp.int32),
            pltpu.SMEM((6, NB), jnp.int32),
            pltpu.SMEM((3, NB), jnp.int32),
            pltpu.SMEM((3, TAPS), f32),
            pltpu.VMEM(observed.shape, f32),
            pltpu.VMEM(estimate.shape, f32),
            pltpu.SemaphoreType.DMA((6,)),
            pltpu.VMEM((256, 128), f32),
            pltpu.VMEM(estimate.shape, f32),
            pltpu.VMEM(estimate.shape, f32),
            pltpu.SemaphoreType.DMA((3,)),
        ],
        compiler_params=pltpu.CompilerParams(
            collective_id=0, has_side_effects=True
        ),
        name="splitting_step",
    )(slot_brick, neighbours.T, coords.T, blur_taps, observed, estimate)
    return pl.pallas_call(
        hand_over,
        out_shape=(shape, shape),
        in_specs=[place] * 2,
        out_specs=(place, place),
        scratch_shapes=[
            pltpu.VMEM((2, *estimate.shape), f32),
            pltpu.SemaphoreType.DMA((8,)),
            pltpu.SemaphoreType.DMA((8,)),
        ],
        name="hand_over",
    )(*found)


def solution(mesh):
    split = P("bricks", "slab", None, None)
    return jax.shard_map(
        shards,
        mesh=mesh,
        in_specs=(split, split, P(), P(), P(), P()),
        out_specs=(split, split),
        check_vma=False,
    )
```
